512 devices in a mesh: fsdp: 32 (over z_lo, x, core), seq: 16 (over y, z_hi).
Axes of the slice: x: 4, y: 8, z: 8 (z_hi: 2, z_lo: 4; z = z_hi * 4 + z_lo), core: 2. Of those that a mesh axis runs over, the one named last changes fastest.
Arguments:
- streams: bfloat16 [3, 8192, 4096], P(None, 'seq', 'fsdp'), may hold values from -6 to 6
- record_blocks: int32 [3], replicated, may hold values from 1 to 32, as said below
- tail_rows: int32 [3], replicated, may hold values from 1 to 128
- unit_dest: int32 [512], replicated, may hold values from 0 to 511, as said below
- mixer_filter: float32 [128, 4096], P(None, ('fsdp', 'seq')), may hold values from -0.5 to 0.5
- feat_filter: float32 [7, 3, 4096], P(None, None, ('fsdp', 'seq')), may hold values from -2 to 2
- norm_gain: float32 [4096], P(('fsdp', 'seq')), may hold values from 0.25 to 1.75
- out_grad: bfloat16 [8192, 4096], P('seq', 'fsdp'), may hold values from -6 to 6
Outputs:
- out: bfloat16 [8192, 4096], P('seq', 'fsdp')
- stream_grad: bfloat16 [3, 8192, 4096], P(None, 'seq', 'fsdp')
- mixer_grad: float32 [128, 4096], P(None, ('fsdp', 'seq'))
- feat_grad: float32 [7, 3, 4096], P(None, None, ('fsdp', 'seq'))
- gain_grad: float32 [4096], P(('fsdp', 'seq'))
The draws below stay inside these ranges and needn't reach their ends.
Inputs may be any that keep to these rules, and one draw needn't show every extreme that they name: unit_dest is a permutation; the 32 units of each shard of 512 rows go to exactly half of the shards, 4 units to each of them, so each shard receives 4 units from each of half of the shards. record_blocks sums to 64; the second record is the longest, exactly 32 blocks.
All inputs are finite; a program needn't handle non-finite values.
Results may differ from the reference program's by a relative error of at most 0.0085.
Values may be sent and summed in bfloat16 or wider, within the bound.
A program may use at most 64 MiB of HBM per device.

```python
import jax
import jax.numpy as jnp
import numpy as np
from jax import lax

C = 4096
KM = 128
KF = 7
UNIT = 16
RECORDS = 3
T_DEV = 512
TOKENS = 8192
NU = 32
UNITS = 512
CAP = 4
NBLK = 64
MOSTB = 32


def draw_unit_dest(key, part):
    shards = TOKENS // T_DEV
    subkeys = jax.random.split(key, 5)
    source_order = jax.random.permutation(subkeys[0], shards)
    target_order = jax.random.permutation(subkeys[1], shards)
    offsets = jax.random.permutation(subkeys[2], shards)[:shards // 2]
    within = jax.vmap(lambda one_key: jax.random.permutation(one_key, NU))(jax.random.split(subkeys[3], shards))
    offset_index = within // CAP
    rank_in = within % CAP
    target = target_order[(source_order[:, None] + offsets[offset_index]) % shards]
    arrival = jax.vmap(lambda one_key: jax.random.permutation(one_key, NU))(jax.random.split(subkeys[4], shards))
    local_slot = arrival[target, offset_index * CAP + rank_in]
    return (target * NU + local_slot).reshape(-1).astype(jnp.int32)


def draw_record_blocks(key, part):
    own_key = jax.random.fold_in(key, 7321)
    shard_blocks = T_DEV // KM
    first_len = jax.random.randint(own_key, (1,), shard_blocks + 1, NBLK // 2).astype(jnp.int32)
    long_len = jnp.full((1,), MOSTB, jnp.int32)
    last_len = (NBLK - MOSTB - first_len).astype(jnp.int32)
    return jnp.concatenate([first_len, long_len, last_len]).astype(jnp.int32)


def shard_levels(stream_key, dims, cuts, smallest, top_value):
    def one(axis_at, blocks):
        draws = jax.random.uniform(jax.random.fold_in(jax.random.fold_in(stream_key, 6), axis_at), (blocks,), jnp.float32, smallest / len(cuts), top_value / len(cuts))
        return jnp.repeat(jnp.exp(draws), dims[axis_at] // blocks).reshape((-1,) + (1,) * (len(dims) - axis_at - 1))

    level = one(*cuts[0])
    for cut in cuts[1:]:
        level = level * one(*cut)
    return level


def scatter_about(rng, dims, width, limit, cuts=(), held_as=jnp.bfloat16):
    array = jax.random.normal(rng, dims, jnp.float32) * width
    if len(cuts) > 0:
        array = shard_levels(rng, dims, cuts, -0.22, 0.18) * array
    return jnp.clip(array, min=-limit, max=limit).astype(held_as)


def setup_inputs(seed: int = 0) -> dict:
    splits = jax.random.split(jax.random.key(seed), 9)
    return {
        "streams": scatter_about(splits[0], (3, TOKENS, C), 1.0, 6.0, ((1, 16), (2, 32))),
        "record_blocks": draw_record_blocks(jax.random.fold_in(splits[8], 71), 0),
        "tail_rows": jax.random.randint(splits[2], (RECORDS,), 1, KM + 1).astype(jnp.int32),
        "unit_dest": draw_unit_dest(jax.random.fold_in(splits[8], 71), 0),
        "mixer_filter": scatter_about(splits[4], (KM, C), 0.09, 0.5, ((1, 512),), jnp.float32),
        "feat_filter": scatter_about(splits[5], (KF, 3, C), 0.38, 2.0, ((2, 512),), jnp.float32),
        "norm_gain": jnp.clip(1.0 + 0.15 * jax.random.normal(splits[6], (C,), jnp.float32), 0.25, 1.75),
        "out_grad": scatter_about(splits[7], (TOKENS, C), 1.0, 6.0, ((0, 16), (1, 32))),
    }


EPSILON = 1e-06

def lag_table(length):
    row_index = np.arange(length)[:, None]
    col_index = np.arange(2 * length)[None, :]
    lagged = length + row_index - col_index
    return np.where((lagged >= 0) & (lagged < length), lagged, length).astype(np.int32)

def toeplitz(filter_bf):
    padded = jnp.concatenate([filter_bf.T, jnp.zeros((filter_bf.shape[1], 1), filter_bf.dtype)], axis=1)
    return jnp.take(padded, jnp.asarray(lag_table(filter_bf.shape[0])), axis=1)

def record_masks(record_blocks, tail_rows, first_block, block_count):
    starts = jnp.cumsum(record_blocks).astype(jnp.int32) - record_blocks
    record_ends = starts + record_blocks - 1
    block_ids = first_block + jnp.arange(block_count, dtype=jnp.int32)
    starts_here = jnp.any(starts[None, :] == block_ids[:, None], axis=1)
    starts_next = jnp.any(starts[None, :] == block_ids[:, None] + 1, axis=1)
    closing = record_ends[None, :] == block_ids[:, None]
    filled_rows = jnp.where(jnp.any(closing, axis=1), lax.optimization_barrier(jnp.sum(jnp.where(closing, tail_rows[None, :], 0), axis=1)), KM)
    live_rows = (jnp.arange(KM, dtype=jnp.int32)[None, :] < filled_rows[:, None]).astype(jnp.float32)
    carry_on = 1.0 - starts_here.astype(jnp.float32)
    carry_next = 1.0 - starts_next.astype(jnp.float32)
    return (carry_on, carry_next, live_rows)

def featurize(extended, feat_taps, live_rows):
    accumulated = jnp.zeros(extended.shape[:2] + (KM, extended.shape[3]), jnp.float32)
    for tap_index in range(KF):
        window = extended[:, :, 8 - tap_index:8 - tap_index + KM].astype(jnp.float32)
        accumulated = accumulated + feat_taps[tap_index][:, None, None, :] * window
    return (accumulated * live_rows[None, :, :, None]).astype(jnp.bfloat16)

def spread(d_extended, feat_taps):
    accumulated = jnp.zeros(d_extended.shape[:2] + (KM, d_extended.shape[3]), jnp.float32)
    for tap_index in range(KF):
        window = d_extended[:, :, tap_index:tap_index + KM].astype(jnp.float32)
        accumulated = accumulated + feat_taps[tap_index][:, None, None, :] * window
    return accumulated.astype(jnp.bfloat16)

def tap_sums(d_feature, extended):
    d_float = d_feature.astype(jnp.float32)
    collected = []
    for tap_index in range(KF):
        window = extended[:, :, 8 - tap_index:8 - tap_index + KM].astype(jnp.float32)
        collected.append(lax.optimization_barrier(jnp.sum(d_float * window, axis=(1, 2))))
    return jnp.stack(collected)

def lag_sums(d_response, both_parts):
    products = jnp.einsum('bic,bkc->cik', d_response.astype(jnp.float32), both_parts.astype(jnp.float32))
    group_width = products.shape[0]
    flattened = jnp.pad(products.reshape(group_width, 2 * KM * KM), ((0, 0), (0, KM)))
    skewed = flattened.reshape(group_width, KM, 2 * KM + 1)
    summed = lax.optimization_barrier(jnp.sum(skewed[:, :, 1:KM + 1], axis=1))
    return summed[:, ::-1].T

def forward_group(packed_group, feat_taps, mixer_taps, carry_on, live_rows):
    block_count = carry_on.shape[0]
    group_width = packed_group.shape[2]
    blocks = packed_group.reshape(3, block_count, KM, group_width)
    zero_tail = jnp.zeros((3, 1, 8, group_width), blocks.dtype)
    tail_part = jnp.concatenate([zero_tail, blocks[:, :-1, KM - 8:]], axis=1)
    tail_part = jnp.where(carry_on[None, :, None, None] > 0, tail_part, jnp.zeros_like(tail_part))
    extended = jnp.concatenate([tail_part, blocks], axis=2)
    feature = featurize(extended, feat_taps, live_rows)
    mixed_in = (feature[1].astype(jnp.float32) * feature[2].astype(jnp.float32)).astype(jnp.bfloat16)
    previous = jnp.concatenate([jnp.zeros((1, KM, group_width), mixed_in.dtype), mixed_in[:-1]], axis=0)
    previous = jnp.where(carry_on[:, None, None] > 0, previous, jnp.zeros_like(previous))
    matrix = toeplitz(mixer_taps.astype(jnp.bfloat16)).astype(jnp.float32)
    response = jnp.einsum('cik,bkc->bic', matrix[:, :, KM:], mixed_in.astype(jnp.float32))
    response = response + jnp.einsum('cik,bkc->bic', matrix[:, :, :KM], previous.astype(jnp.float32))
    gated_out = (feature[0].astype(jnp.float32) * response).astype(jnp.bfloat16)
    return (extended, feature, mixed_in, previous, matrix, response, gated_out)

def backward_group(packed_group, feat_taps, mixer_taps, d_gated, carry_on, carry_next, live_rows):
    extended, feature, mixed_in, previous, matrix, response, unused_out = forward_group(packed_group, feat_taps, mixer_taps, carry_on, live_rows)
    group_width = packed_group.shape[2]
    d_gated_float = d_gated.astype(jnp.float32)
    d_query = d_gated_float * response
    d_response = (d_gated_float * feature[0].astype(jnp.float32)).astype(jnp.bfloat16)
    following = jnp.concatenate([d_response[1:], jnp.zeros((1, KM, group_width), d_response.dtype)], axis=0)
    following = jnp.where(carry_next[:, None, None] > 0, following, jnp.zeros_like(following))
    d_mixed = jnp.einsum('cik,bic->bkc', matrix[:, :, KM:], d_response.astype(jnp.float32))
    d_mixed = d_mixed + jnp.einsum('cik,bic->bkc', matrix[:, :, :KM], following.astype(jnp.float32))
    d_feature = jnp.stack([d_query, d_mixed * feature[2].astype(jnp.float32), d_mixed * feature[1].astype(jnp.float32)]).astype(jnp.bfloat16)
    mixer_part = lag_sums(d_response, jnp.concatenate([previous, mixed_in], axis=1))
    feat_part = tap_sums(d_feature, extended)
    head_rows = jnp.concatenate([d_feature[:, 1:, :8], jnp.zeros((3, 1, 8, group_width), d_feature.dtype)], axis=1)
    head_rows = jnp.where(carry_next[None, :, None, None] > 0, head_rows, jnp.zeros_like(head_rows))
    d_extended = jnp.concatenate([d_feature, head_rows], axis=2)
    return (spread(d_extended, feat_taps), mixer_part, feat_part)

def reference(streams, record_blocks, tail_rows, unit_dest, mixer_filter, feat_filter, norm_gain, out_grad):
    unit_rows = streams.reshape(3, UNITS, UNIT, C)
    inverse = jnp.zeros((UNITS,), jnp.int32).at[unit_dest].set(jnp.arange(UNITS, dtype=jnp.int32))
    packed = jnp.take(unit_rows, inverse, axis=1).reshape(3, TOKENS, C)
    carry_on, carry_next, live_rows = record_masks(record_blocks, tail_rows, 0, NBLK)
    group_width = min(128, C)
    group_count = C // group_width
    packed_groups = packed.reshape(3, TOKENS, group_count, group_width).transpose(2, 0, 1, 3)
    feat_groups = feat_filter.reshape(KF, 3, group_count, group_width).transpose(2, 0, 1, 3)
    mixer_groups = mixer_filter.reshape(KM, group_count, group_width).transpose(1, 0, 2)

    def first_pass(operands):
        return forward_group(operands[0], operands[1], operands[2], carry_on, live_rows)[6]
    gated_groups = lax.map(first_pass, (packed_groups, feat_groups, mixer_groups))
    gated_out = gated_groups.transpose(1, 2, 0, 3).reshape(NBLK, KM, C)
    squares = lax.optimization_barrier(jnp.sum(jnp.square(gated_out.astype(jnp.float32)), axis=-1))
    row_scale = live_rows * lax.rsqrt(squares / C + EPSILON)
    normed = gated_out.astype(jnp.float32) * row_scale[..., None]
    out = (normed * norm_gain).astype(jnp.bfloat16).reshape(TOKENS, C)
    grad_rows = out_grad.reshape(NBLK, KM, C).astype(jnp.float32)
    gain_grad = lax.optimization_barrier(jnp.sum(grad_rows * normed, axis=(0, 1)))
    weighted = grad_rows * norm_gain
    inner_sum = lax.optimization_barrier(jnp.sum(weighted * normed, axis=-1)) / C
    d_gated = (row_scale[..., None] * (weighted - normed * inner_sum[..., None])).astype(jnp.bfloat16)
    d_groups = d_gated.reshape(NBLK, KM, group_count, group_width).transpose(2, 0, 1, 3)

    def second_pass(operands):
        return backward_group(operands[0], operands[1], operands[2], operands[3], carry_on, carry_next, live_rows)
    d_packed, mixer_parts, feat_parts = lax.map(second_pass, (packed_groups, feat_groups, mixer_groups, d_groups))
    d_packed = d_packed.transpose(1, 2, 3, 0, 4).reshape(3, UNITS, UNIT, C)
    stream_grad = jnp.take(d_packed, unit_dest, axis=1).reshape(3, TOKENS, C)
    mixer_grad = mixer_parts.transpose(1, 0, 2).reshape(KM, C)
    feat_grad = feat_parts.transpose(1, 2, 0, 3).reshape(KF, 3, C)
    return (out, stream_grad, mixer_grad, feat_grad, gain_grad)
```

```python
import functools

import jax
import jax.numpy as jnp
from jax import lax
from jax.experimental import pallas as pl
from jax.experimental.pallas import tpu as pltpu
from jax.sharding import PartitionSpec as P

C = 4096
KM = 128
KF = 7
UNIT = 16
CAP = 4
EPSILON = 1e-06
INTERPRET = False

F32 = jnp.float32
BF16 = jnp.bfloat16
VMEM = pl.BlockSpec(memory_space=pltpu.VMEM)
SMEM = pl.BlockSpec(memory_space=pltpu.SMEM)

LANES = 128
BLOCKS = 4
ROWS = BLOCKS * KM
SHARDS = 16
UNITS_DEV = ROWS // UNIT
OUT_UNITS = 3 * CAP + 1
BACK_UNITS = 3 * CAP + 2
RIM = KM + 3 * UNIT


def call(kernel, out_shape, scratch, *operands, scalars=0):
    return pl.pallas_call(
        kernel,
        out_shape=out_shape,
        in_specs=[SMEM] * scalars + [VMEM] * (len(operands) - scalars),
        out_specs=jax.tree.map(lambda _: VMEM, out_shape),
        scratch_shapes=scratch,
        interpret=INTERPRET,
    )(*operands)


def shape(*dims, dtype=BF16):
    return jax.ShapeDtypeStruct(dims, dtype)


def parts_of(value):
    high = value.astype(BF16).astype(F32)
    rest = value - high
    middle = rest.astype(BF16).astype(F32)
    return high, middle, rest - middle


def block_facts(records, tails, block):
    second = records[0]
    third = records[0] + records[1]
    end = third + records[2]

    def begins(index):
        return (index == 0) | (index == second) | (index == third)

    used = jnp.where(
        block + 1 == second,
        tails[0],
        jnp.where(block + 1 == third, tails[1], jnp.where(block + 1 == end, tails[2], KM)),
    )
    carry = jnp.where(begins(block), 0.0, 1.0).astype(F32)
    carry_next = jnp.where(begins(block + 1) | (block + 1 == end), 0.0, 1.0).astype(F32)
    return carry, carry_next, used


def live_column(used):
    rows = lax.broadcasted_iota(jnp.int32, (KM, LANES), 0)
    return (rows < used).astype(F32)


def fold8(value):
    return jnp.sum(value.reshape(-1, 8, LANES), axis=0)


def pack_kernel(slot, streams, filters, out):
    taps = filters[...]
    high, middle, low = parts_of(taps[:, KM:])
    lane = lax.broadcasted_iota(jnp.int32, (8, LANES), 1)
    small = jnp.where(
        lane < 32,
        high,
        jnp.where(
            lane < 64,
            pltpu.roll(middle, 32, 1),
            jnp.where(lane < 96, pltpu.roll(low, 64, 1), 0.0),
        ),
    )
    panel = jnp.concatenate([taps[:, :KM], small], axis=0).astype(BF16)

    def give(shard, carry):
        out[shard, pl.ds(3 * CAP * UNIT, UNIT), :] = panel
        return carry

    lax.fori_loop(0, SHARDS, give, 0)

    def move(unit, carry):
        to = slot[unit]
        shard = to // CAP
        rank = to % CAP
        for s in range(3):
            out[shard, pl.ds(pl.multiple_of((s * CAP + rank) * UNIT, UNIT), UNIT), :] = streams[
                s, pl.ds(pl.multiple_of(unit * UNIT, UNIT), UNIT), :
            ]
        return carry

    lax.fori_loop(0, UNITS_DEV, move, 0)


def unpack_kernel(slot, records, tails, position, arrived, packed, mixer, small, rim, turned):
    def move(unit, carry):
        at = slot[unit]
        shard = at // CAP
        rank = at % CAP
        for s in range(3):
            packed[s, pl.ds(pl.multiple_of(unit * UNIT, UNIT), UNIT), :] = arrived[
                shard, pl.ds(pl.multiple_of((s * CAP + rank) * UNIT, UNIT), UNIT), :
            ]
        return carry

    lax.fori_loop(0, UNITS_DEV, move, 0)
    for shard in range(SHARDS):
        panel = arrived[shard, 3 * CAP * UNIT :, :].astype(F32)
        turned[0, shard * 8 : shard * 8 + 8, :] = panel[:8]
        turned[1, shard * 8 : shard * 8 + 8, :] = panel[8:]
    mixer[...] = turned[0].T
    pieces = turned[1].T
    small[...] = pieces[0:32] + pieces[32:64] + pieces[64:96]

    _, _, used = block_facts(records, tails, position[0] * BLOCKS + BLOCKS - 1)
    live = live_column(used)
    both = []
    for s in (1, 2):
        wide = packed[s, ROWS - KM - UNIT :, :].astype(F32)
        total = jnp.zeros((KM, LANES), F32)
        for tap in range(KF):
            row = tap * 3 + s
            total = total + small[row : row + 1, :] * wide[UNIT - tap : UNIT - tap + KM]
        both.append((total * live).astype(BF16).astype(F32))
    rim[:KM, :] = (both[0] * both[1]).astype(BF16)
    carry, _, _ = block_facts(records, tails, position[0] * BLOCKS + BLOCKS - 1)

    @pl.when(carry == 0.0)
    def _():
        heads = []
        for s in (1, 2):
            wide = packed[s, ROWS - KM - UNIT : ROWS - KM + UNIT, :].astype(F32)
            rows = lax.broadcasted_iota(jnp.int32, (2 * UNIT, LANES), 0)
            wide = jnp.where(rows < UNIT, 0.0, wide)
            total = jnp.zeros((UNIT, LANES), F32)
            for tap in range(KF):
                row = tap * 3 + s
                total = total + small[row : row + 1, :] * wide[UNIT - tap : 2 * UNIT - tap]
            heads.append((total * live[:UNIT]).astype(BF16).astype(F32))
        rim[:UNIT, :] = (heads[0] * heads[1]).astype(BF16)

    for s in range(3):
        rim[KM + s * UNIT : KM + (s + 1) * UNIT, :] = packed[s, ROWS - UNIT :, :]


def forward_kernel(
    records,
    tails,
    position,
    packed,
    rim,
    mixer,
    small,
    out_grad,
    feature,
    response,
    sums,
    window,
    mixed,
    pair,
    shifted,
):
    first = position[0] * BLOCKS
    mixed[:KM, :] = rim[:KM, :].astype(F32)
    for b in range(BLOCKS):
        carry, _, used = block_facts(records, tails, first + b)
        live = live_column(used)
        both = []
        for s in range(3):
            if b == 0:
                tail = rim[KM + s * UNIT : KM + (s + 1) * UNIT, :].astype(F32)
            else:
                tail = packed[s, b * KM - UNIT : b * KM, :].astype(F32)
            window[s, :UNIT, :] = tail * carry
            window[s, UNIT:, :] = packed[s, b * KM : (b + 1) * KM, :].astype(F32)
            total = jnp.zeros((KM, LANES), F32)
            for tap in range(KF):
                row = tap * 3 + s
                total = total + small[row : row + 1, :] * window[s, UNIT - tap : UNIT - tap + KM, :]
            rounded = (total * live).astype(BF16)
            feature[s, b * KM : (b + 1) * KM, :] = rounded
            both.append(rounded.astype(F32))
        mixed[(b + 1) * KM : (b + 2) * KM, :] = (both[1] * both[2]).astype(BF16).astype(F32)

    gain = small[21:22, :]
    ones = jnp.ones((8, LANES), F32)
    line = lax.broadcasted_iota(jnp.int32, (8, LANES), 0)

    def one_block(b, collected):
        carry, _, _ = block_facts(records, tails, first + b)
        here = pl.ds(pl.multiple_of(b * KM, KM), KM)
        pair[:KM, :] = mixed[here, :] * carry
        pair[KM:, :] = mixed[pl.ds(pl.multiple_of((b + 1) * KM, KM), KM), :]
        for s in range(8):
            shifted[s, 8:, :] = pair[8 - s : 2 * KM - s, :]
        total = jnp.zeros((KM, LANES), F32)
        for s in range(8):
            for k in range(16):
                lag = 8 * k + s
                total = total + mixer[lag : lag + 1, :] * shifted[s, KM - 8 * k : 2 * KM - 8 * k, :]
        response[here, :] = total
        gated = (feature[0, here, :].astype(F32) * total).astype(BF16).astype(F32)
        weighted = out_grad[here, :].astype(F32) * gain
        contract = (((1,), (1,)), ((), ()))
        squares = lax.dot_general(
            ones, gated * gated, contract, precision=lax.Precision.HIGHEST,
            preferred_element_type=F32,
        )
        inner = lax.dot_general(
            ones, weighted * gated, contract, precision=lax.Precision.HIGHEST,
            preferred_element_type=F32,
        )
        return jnp.where(line == b, squares, jnp.where(line == b + BLOCKS, inner, collected))

    collected = lax.fori_loop(0, BLOCKS, one_block, jnp.zeros((8, LANES), F32))
    for member in range(sums.shape[0]):
        sums[member] = collected


def middle_kernel(
    records,
    tails,
    position,
    sums,
    feature,
    response,
    mixer,
    small,
    out_grad,
    out,
    query,
    reply,
    gain_sum,
    rim,
    window,
):
    first = position[0] * BLOCKS
    total = jnp.sum(sums[...], axis=0)
    line = lax.broadcasted_iota(jnp.int32, (8, LANES), 0)
    lane = lax.broadcasted_iota(jnp.int32, (8, LANES), 1)
    used = jnp.full((8, LANES), KM, jnp.int32)
    for b in range(BLOCKS):
        _, _, own = block_facts(records, tails, first + b)
        used = jnp.where(line == b, own, used)
    scale = (lane < used).astype(F32) * lax.rsqrt(total / C + EPSILON)
    inner = pltpu.roll(total, BLOCKS, 0) * scale / C
    both = jnp.where(line < BLOCKS, scale, pltpu.roll(inner, BLOCKS, 0))
    columns = jnp.concatenate([both] * 16, axis=0).T
    gain = small[21:22, :]
    gain_total = jnp.zeros((8, LANES), F32)
    for b in range(BLOCKS):
        here = slice(b * KM, (b + 1) * KM)
        scale_b = jnp.broadcast_to(columns[:, b : b + 1], (KM, LANES))
        inner_b = jnp.broadcast_to(columns[:, b + BLOCKS : b + BLOCKS + 1], (KM, LANES))
        query_feature = feature[0, here, :].astype(F32)
        answer = response[here, :]
        gated = (query_feature * answer).astype(BF16).astype(F32)
        normed = gated * scale_b
        out[here, :] = (normed * gain).astype(BF16)
        grad = out_grad[here, :].astype(F32)
        gain_total = gain_total + fold8(grad * normed)
        d_gated = (scale_b * (grad * gain - normed * inner_b)).astype(BF16).astype(F32)
        query[here, :] = (d_gated * answer).astype(BF16)
        reply[here, :] = (d_gated * query_feature).astype(BF16)
    gain_sum[...] = gain_total

    _, carry_next, _ = block_facts(records, tails, first)
    window[:KM, :] = reply[:KM, :].astype(F32)
    window[KM:, :] = reply[KM : KM + UNIT, :].astype(F32) * carry_next
    totals = [jnp.zeros((8, LANES), F32) for _ in range(4)]
    for lag in range(KM):
        totals[lag % 4] = totals[lag % 4] + mixer[lag : lag + 1, :] * window[lag : lag + 8, :]
    d_mixed = (totals[0] + totals[1]) + (totals[2] + totals[3])
    d_mixed = jnp.concatenate([d_mixed, jnp.zeros_like(d_mixed)], axis=0)
    rim[:KM, :] = reply[:KM, :]
    rim[KM : KM + UNIT, :] = query[:UNIT, :]
    rim[KM + UNIT : KM + 2 * UNIT, :] = (d_mixed * feature[2, :UNIT, :].astype(F32)).astype(BF16)
    rim[KM + 2 * UNIT :, :] = (d_mixed * feature[1, :UNIT, :].astype(F32)).astype(BF16)


def backward_kernel(
    slot,
    records,
    tails,
    position,
    query,
    reply,
    rim_back,
    feature,
    packed,
    rim,
    mixer,
    small,
    gain_sum,
    back,
    mixed,
    replies,
    pair,
    shifted,
    lag_total,
    d_feature,
    window,
    tap_total,
    spread,
):
    first = position[0] * BLOCKS
    mixed[:KM, :] = rim[:KM, :].astype(F32)
    replies[ROWS:, :] = rim_back[:KM, :].astype(F32)
    for b in range(BLOCKS):
        here = slice(b * KM, (b + 1) * KM)
        product = feature[1, here, :].astype(F32) * feature[2, here, :].astype(F32)
        mixed[(b + 1) * KM : (b + 2) * KM, :] = product.astype(BF16).astype(F32)
        replies[here, :] = reply[here, :].astype(F32)
    for s in range(3):
        d_feature[s, ROWS:, :] = rim_back[KM + s * UNIT : KM + (s + 1) * UNIT, :].astype(F32)
    d_feature[0, :ROWS, :] = query[...].astype(F32)
    lag_total[...] = jnp.zeros_like(lag_total)

    def one_block(b, unused):
        carry, carry_next, _ = block_facts(records, tails, first + b)
        here = pl.ds(pl.multiple_of(b * KM, KM), KM)
        after = pl.ds(pl.multiple_of((b + 1) * KM, KM), KM)
        pair[:KM, :] = replies[here, :]
        pair[KM:, :] = replies[after, :] * carry_next
        for s in range(8):
            shifted[s, : 2 * KM - 8, :] = pair[s : 2 * KM - 8 + s, :]
        total = jnp.zeros((KM, LANES), F32)
        for s in range(8):
            for k in range(16):
                lag = 8 * k + s
                total = total + mixer[lag : lag + 1, :] * shifted[s, 8 * k : 8 * k + KM, :]
        d_feature[1, here, :] = (total * feature[2, here, :].astype(F32)).astype(BF16).astype(F32)
        d_feature[2, here, :] = (total * feature[1, here, :].astype(F32)).astype(BF16).astype(F32)
        pair[:KM, :] = mixed[here, :] * carry
        pair[KM:, :] = mixed[after, :]
        for s in range(8):
            shifted[s, 8:, :] = pair[8 - s : 2 * KM - s, :]
        own = replies[here, :]
        for s in range(8):
            for k in range(16):
                lag = 8 * k + s
                lag_total[lag] = lag_total[lag] + fold8(
                    own * shifted[s, KM - 8 * k : 2 * KM - 8 * k, :]
                )
        return unused

    lax.fori_loop(0, BLOCKS, one_block, 0)

    tap_total[...] = jnp.zeros_like(tap_total)
    for b in range(BLOCKS):
        carry, carry_next, _ = block_facts(records, tails, first + b)
        here = slice(b * KM, (b + 1) * KM)
        for s in range(3):
            if b == 0:
                tail = rim[KM + s * UNIT : KM + (s + 1) * UNIT, :].astype(F32)
            else:
                tail = packed[s, b * KM - UNIT : b * KM, :].astype(F32)
            window[:UNIT, :] = tail * carry
            window[UNIT:, :] = packed[s, here, :].astype(F32)
            own = d_feature[s, here, :]
            for tap in range(KF):
                row = tap * 3 + s
                tap_total[row] = tap_total[row] + fold8(own * window[UNIT - tap : UNIT - tap + KM, :])
            window[:KM, :] = own
            window[KM:, :] = d_feature[s, (b + 1) * KM : (b + 1) * KM + UNIT, :] * carry_next
            total = jnp.zeros((KM, LANES), F32)
            for tap in range(KF):
                row = tap * 3 + s
                total = total + small[row : row + 1, :] * window[tap : tap + KM, :]
            spread[s, here, :] = total.astype(BF16)

    tap_total[21] = gain_sum[...]
    mixer_parts = parts_of(jnp.sum(lag_total[...], axis=1).T)
    small_parts = parts_of(jnp.sum(tap_total[...], axis=1))
    rest = jnp.zeros((KM - 96, LANES), F32)
    turned = jnp.concatenate(list(small_parts) + [rest], axis=0).T
    for shard in range(SHARDS):
        rows = slice(shard * 8, shard * 8 + 8)
        pieces = jnp.concatenate([part[rows] for part in mixer_parts] + [turned[rows]], axis=0)
        back[shard, 3 * CAP * UNIT :, :] = pieces.astype(BF16)

    def move(unit, carry):
        to = slot[unit]
        shard = to // CAP
        rank = to % CAP
        for s in range(3):
            back[shard, pl.ds(pl.multiple_of((s * CAP + rank) * UNIT, UNIT), UNIT), :] = spread[
                s, pl.ds(pl.multiple_of(unit * UNIT, UNIT), UNIT), :
            ]
        return carry

    lax.fori_loop(0, UNITS_DEV, move, 0)


def finish_kernel(slot, returned, stream_grad, grads):
    def move(unit, carry):
        at = slot[unit]
        shard = at // CAP
        rank = at % CAP
        for s in range(3):
            stream_grad[s, pl.ds(pl.multiple_of(unit * UNIT, UNIT), UNIT), :] = returned[
                shard, pl.ds(pl.multiple_of((s * CAP + rank) * UNIT, UNIT), UNIT), :
            ]
        return carry

    lax.fori_loop(0, UNITS_DEV, move, 0)
    total = jnp.zeros((2 * UNIT, LANES), F32)
    for shard in range(SHARDS):
        total = total + returned[shard, 3 * CAP * UNIT :, :].astype(F32)
    grads[:, :KM] = total[0:8] + total[8:16] + total[16:24]
    pieces = total[24:32]
    grads[:, KM:] = pieces + pltpu.roll(pieces, LANES - 32, 1) + pltpu.roll(pieces, LANES - 64, 1)


def routing(unit_dest, position):
    target = (unit_dest // UNITS_DEV).reshape(SHARDS, UNITS_DEV)
    ids = jnp.arange(UNITS_DEV, dtype=jnp.int32)
    same = (target[:, :, None] == target[:, None, :]) & (ids[None, :] < ids[:, None])[None]
    rank = jnp.sum(same.astype(jnp.int32), axis=2)
    own_slot = lax.dynamic_index_in_dim(target * CAP + rank, position, 0, keepdims=False)
    arrive = (jnp.arange(SHARDS, dtype=jnp.int32)[:, None] * CAP + rank).reshape(-1)
    match = unit_dest[None, :] == (position * UNITS_DEV + ids)[:, None]
    packed_slot = jnp.sum(jnp.where(match, arrive[None, :], 0), axis=1)
    return own_slot.astype(jnp.int32), packed_slot.astype(jnp.int32)


def body(
    streams, record_blocks, tail_rows, unit_dest, mixer_filter, feat_filter, norm_gain, out_grad
):
    members = lax.axis_size("fsdp")
    position = lax.axis_index("seq").astype(jnp.int32)
    own_slot, packed_slot = routing(unit_dest, position)
    where = position.reshape(1)
    filters = jnp.concatenate(
        [
            mixer_filter,
            feat_filter.reshape(KF * 3, 8),
            norm_gain.reshape(1, 8),
            jnp.zeros((LANES - KF * 3 - 1, 8), F32),
        ],
        axis=0,
    ).T
    outgoing = call(
        pack_kernel,
        shape(SHARDS, OUT_UNITS * UNIT, LANES),
        [],
        own_slot,
        streams,
        filters,
        scalars=1,
    )
    arrived = lax.all_to_all(outgoing, "seq", split_axis=0, concat_axis=0, tiled=True)
    facts = (record_blocks, tail_rows, where)
    packed, mixer, small, rim_out = call(
        unpack_kernel,
        (
            shape(3, ROWS, LANES),
            shape(KM, LANES, dtype=F32),
            shape(32, LANES, dtype=F32),
            shape(RIM, LANES),
        ),
        [pltpu.VMEM((2, LANES, LANES), F32)],
        packed_slot,
        *facts,
        arrived,
        scalars=4,
    )
    rim = lax.ppermute(rim_out, "seq", [(i, i + 1) for i in range(SHARDS - 1)])
    feature, response, sums = call(
        forward_kernel,
        (
            shape(3, ROWS, LANES),
            shape(ROWS, LANES, dtype=F32),
            shape(members, 8, LANES, dtype=F32),
        ),
        [
            pltpu.VMEM((3, UNIT + KM, LANES), F32),
            pltpu.VMEM((ROWS + KM, LANES), F32),
            pltpu.VMEM((2 * KM, LANES), F32),
            pltpu.VMEM((8, 2 * KM, LANES), F32),
        ],
        *facts,
        packed,
        rim,
        mixer,
        small,
        out_grad,
        scalars=3,
    )
    sums = lax.all_to_all(sums, "fsdp", split_axis=0, concat_axis=0, tiled=True)
    out, query, reply, gain_sum, rim_back_out = call(
        middle_kernel,
        (
            shape(ROWS, LANES),
            shape(ROWS, LANES),
            shape(ROWS, LANES),
            shape(8, LANES, dtype=F32),
            shape(RIM, LANES),
        ),
        [pltpu.VMEM((KM + UNIT, LANES), F32)],
        *facts,
        sums,
        feature,
        response,
        mixer,
        small,
        out_grad,
        scalars=3,
    )
    rim_back = lax.ppermute(rim_back_out, "seq", [(i + 1, i) for i in range(SHARDS - 1)])
    returning = call(
        backward_kernel,
        shape(SHARDS, BACK_UNITS * UNIT, LANES),
        [
            pltpu.VMEM((ROWS + KM, LANES), F32),
            pltpu.VMEM((ROWS + KM, LANES), F32),
            pltpu.VMEM((2 * KM, LANES), F32),
            pltpu.VMEM((8, 2 * KM, LANES), F32),
            pltpu.VMEM((KM, 8, LANES), F32),
            pltpu.VMEM((3, ROWS + UNIT, LANES), F32),
            pltpu.VMEM((KM + UNIT, LANES), F32),
            pltpu.VMEM((32, 8, LANES), F32),
            pltpu.VMEM((3, ROWS, LANES), BF16),
        ],
        packed_slot,
        *facts,
        query,
        reply,
        rim_back,
        feature,
        packed,
        rim,
        mixer,
        small,
        gain_sum,
        scalars=4,
    )
    returned = lax.all_to_all(returning, "seq", split_axis=0, concat_axis=0, tiled=True)
    stream_grad, grads = call(
        finish_kernel,
        (shape(3, ROWS, LANES), shape(8, 2 * LANES, dtype=F32)),
        [],
        own_slot,
        returned,
        scalars=1,
    )
    turned = grads.T
    mixer_grad = turned[:KM]
    feat_grad = turned[KM : KM + KF * 3].reshape(KF, 3, 8)
    gain_grad = turned[KM + KF * 3]
    return (out, stream_grad, mixer_grad, feat_grad, gain_grad)


def solution(mesh):
    placed = (
        P(None, "seq", "fsdp"),
        P(),
        P(),
        P(),
        P(None, ("fsdp", "seq")),
        P(None, None, ("fsdp", "seq")),
        P(("fsdp", "seq")),
        P("seq", "fsdp"),
    )
    return jax.shard_map(
        body,
        mesh=mesh,
        in_specs=placed,
        out_specs=(
            P("seq", "fsdp"),
            P(None, "seq", "fsdp"),
            P(None, ("fsdp", "seq")),
            P(None, None, ("fsdp", "seq")),
            P(("fsdp", "seq")),
        ),
        check_vma=False,
    )
```

```python
import functools

import jax
import jax.numpy as jnp
from jax import lax
from jax.experimental import pallas as pl
from jax.experimental.pallas import tpu as pltpu
from jax.sharding import PartitionSpec as P

C = 4096
KM = 128
KF = 7
UNIT = 16
CAP = 4
EPSILON = 1e-06
INTERPRET = False

F32 = jnp.float32
BF16 = jnp.bfloat16
VMEM = pl.BlockSpec(memory_space=pltpu.VMEM)
SMEM = pl.BlockSpec(memory_space=pltpu.SMEM)

LANES = 128
BLOCKS = 4
ROWS = BLOCKS * KM
SHARDS = 16
UNITS_DEV = ROWS // UNIT
OUT_UNITS = 3 * CAP + 1
BACK_UNITS = 3 * CAP + 2
RIM = KM + 3 * UNIT


def call(kernel, out_shape, scratch, *operands, scalars=0):
    return pl.pallas_call(
        kernel,
        out_shape=out_shape,
        in_specs=[SMEM] * scalars + [VMEM] * (len(operands) - scalars),
        out_specs=jax.tree.map(lambda _: VMEM, out_shape),
        scratch_shapes=scratch,
        interpret=INTERPRET,
    )(*operands)


def shape(*dims, dtype=BF16):
    return jax.ShapeDtypeStruct(dims, dtype)


def parts_of(value):
    high = value.astype(BF16).astype(F32)
    rest = value - high
    middle = rest.astype(BF16).astype(F32)
    return high, middle, rest - middle


def block_facts(records, tails, block):
    second = records[0]
    third = records[0] + records[1]
    end = third + records[2]

    def begins(index):
        return (index == 0) | (index == second) | (index == third)

    used = jnp.where(
        block + 1 == second,
        tails[0],
        jnp.where(block + 1 == third, tails[1], jnp.where(block + 1 == end, tails[2], KM)),
    )
    carry = jnp.where(begins(block), 0.0, 1.0).astype(F32)
    carry_next = jnp.where(begins(block + 1) | (block + 1 == end), 0.0, 1.0).astype(F32)
    return carry, carry_next, used


def live_column(used):
    rows = lax.broadcasted_iota(jnp.int32, (KM, LANES), 0)
    return (rows < used).astype(F32)


def fold8(value):
    return jnp.sum(value.reshape(-1, 8, LANES), axis=0)


def pack_kernel(slot, streams, filters, out):
    taps = filters[...]
    high, middle, low = parts_of(taps[:, KM:])
    lane = lax.broadcasted_iota(jnp.int32, (8, LANES), 1)
    small = jnp.where(
        lane < 32,
        high,
        jnp.where(
            lane < 64,
            pltpu.roll(middle, 32, 1),
            jnp.where(lane < 96, pltpu.roll(low, 64, 1), 0.0),
        ),
    )
    panel = jnp.concatenate([taps[:, :KM], small], axis=0).astype(BF16)

    def give(shard, carry):
        out[shard, pl.ds(3 * CAP * UNIT, UNIT), :] = panel
        return carry

    lax.fori_loop(0, SHARDS, give, 0)

    def move(unit, carry):
        to = slot[unit]
        shard = to // CAP
        rank = to % CAP
        for s in range(3):
            out[shard, pl.ds(pl.multiple_of((s * CAP + rank) * UNIT, UNIT), UNIT), :] = streams[
                s, pl.ds(pl.multiple_of(unit * UNIT, UNIT), UNIT), :
            ]
        return carry

    lax.fori_loop(0, UNITS_DEV, move, 0)


def unpack_kernel(slot, records, tails, position, arrived, packed, mixer, small, rim, turned):
    def move(unit, carry):
        at = slot[unit]
        shard = at // CAP
        rank = at % CAP
        for s in range(3):
            packed[s, pl.ds(pl.multiple_of(unit * UNIT, UNIT), UNIT), :] = arrived[
                shard, pl.ds(pl.multiple_of((s * CAP + rank) * UNIT, UNIT), UNIT), :
            ]
        return carry

    lax.fori_loop(0, UNITS_DEV, move, 0)
    for shard in range(SHARDS):
        panel = arrived[shard, 3 * CAP * UNIT :, :].astype(F32)
        turned[0, shard * 8 : shard * 8 + 8, :] = panel[:8]
        turned[1, shard * 8 : shard * 8 + 8, :] = panel[8:]
    mixer[...] = turned[0].T
    pieces = turned[1].T
    small[...] = pieces[0:32] + pieces[32:64] + pieces[64:96]

    _, _, used = block_facts(records, tails, position[0] * BLOCKS + BLOCKS - 1)
    live = live_column(used)
    both = []
    for s in (1, 2):
        wide = packed[s, ROWS - KM - UNIT :, :].astype(F32)
        total = jnp.zeros((KM, LANES), F32)
        for tap in range(KF):
            row = tap * 3 + s
            total = total + small[row : row + 1, :] * wide[UNIT - tap : UNIT - tap + KM]
        both.append((total * live).astype(BF16).astype(F32))
    rim[:KM, :] = (both[0] * both[1]).astype(BF16)
    carry, _, _ = block_facts(records, tails, position[0] * BLOCKS + BLOCKS - 1)

    @pl.when(carry == 0.0)
    def _():
        heads = []
        for s in (1, 2):
            wide = packed[s, ROWS - KM - UNIT : ROWS - KM + UNIT, :].astype(F32)
            rows = lax.broadcasted_iota(jnp.int32, (2 * UNIT, LANES), 0)
            wide = jnp.where(rows < UNIT, 0.0, wide)
            total = jnp.zeros((UNIT, LANES), F32)
            for tap in range(KF):
                row = tap * 3 + s
                total = total + small[row : row + 1, :] * wide[UNIT - tap : 2 * UNIT - tap]
            heads.append((total * live[:UNIT]).astype(BF16).astype(F32))
        rim[:UNIT, :] = (heads[0] * heads[1]).astype(BF16)

    for s in range(3):
        rim[KM + s * UNIT : KM + (s + 1) * UNIT, :] = packed[s, ROWS - UNIT :, :]


def forward_kernel(
    records,
    tails,
    position,
    packed,
    rim,
    mixer,
    small,
    out_grad,
    feature,
    response,
    sums,
    window,
    mixed,
    pair,
    shifted,
):
    first = position[0] * BLOCKS
    mixed[:KM, :] = rim[:KM, :].astype(F32)
    for b in range(BLOCKS):
        carry, _, used = block_facts(records, tails, first + b)
        live = live_column(used)
        both = []
        for s in range(3):
            if b == 0:
                tail = rim[KM + s * UNIT : KM + (s + 1) * UNIT, :].astype(F32)
            else:
                tail = packed[s, b * KM - UNIT : b * KM, :].astype(F32)
            window[s, :UNIT, :] = tail * carry
            window[s, UNIT:, :] = packed[s, b * KM : (b + 1) * KM, :].astype(F32)
            total = jnp.zeros((KM, LANES), F32)
            for tap in range(KF):
                row = tap * 3 + s
                total = total + small[row : row + 1, :] * window[s, UNIT - tap : UNIT - tap + KM, :]
            rounded = (total * live).astype(BF16)
            feature[s, b * KM : (b + 1) * KM, :] = rounded
            both.append(rounded.astype(F32))
        mixed[(b + 1) * KM : (b + 2) * KM, :] = (both[1] * both[2]).astype(BF16).astype(F32)

    gain = small[21:22, :]
    ones = jnp.ones((8, LANES), F32)
    line = lax.broadcasted_iota(jnp.int32, (8, LANES), 0)

    def one_block(b, collected):
        carry, _, _ = block_facts(records, tails, first + b)
        here = pl.ds(pl.multiple_of(b * KM, KM), KM)
        pair[:KM, :] = mixed[here, :] * carry
        pair[KM:, :] = mixed[pl.ds(pl.multiple_of((b + 1) * KM, KM), KM), :]
        for s in range(8):
            shifted[s, 8:, :] = pair[8 - s : 2 * KM - s, :]
        total = jnp.zeros((KM, LANES), F32)
        for s in range(8):
            for k in range(16):
                lag = 8 * k + s
                total = total + mixer[lag : lag + 1, :] * shifted[s, KM - 8 * k : 2 * KM - 8 * k, :]
        response[here, :] = total
        gated = (feature[0, here, :].astype(F32) * total).astype(BF16).astype(F32)
        weighted = out_grad[here, :].astype(F32) * gain
        contract = (((1,), (1,)), ((), ()))
        squares = lax.dot_general(
            ones, gated * gated, contract, precision=lax.Precision.HIGHEST,
            preferred_element_type=F32,
        )
        inner = lax.dot_general(
            ones, weighted * gated, contract, precision=lax.Precision.HIGHEST,
            preferred_element_type=F32,
        )
        return jnp.where(line == b, squares, jnp.where(line == b + BLOCKS, inner, collected))

    collected = lax.fori_loop(0, BLOCKS, one_block, jnp.zeros((8, LANES), F32))
    sums[...] = collected


def middle_kernel(
    records,
    tails,
    position,
    sums,
    feature,
    response,
    mixer,
    small,
    out_grad,
    out,
    query,
    reply,
    gain_sum,
    rim,
    window,
):
    first = position[0] * BLOCKS
    total = jnp.sum(sums[...], axis=0)
    line = lax.broadcasted_iota(jnp.int32, (8, LANES), 0)
    lane = lax.broadcasted_iota(jnp.int32, (8, LANES), 1)
    used = jnp.full((8, LANES), KM, jnp.int32)
    for b in range(BLOCKS):
        _, _, own = block_facts(records, tails, first + b)
        used = jnp.where(line == b, own, used)
    scale = (lane < used).astype(F32) * lax.rsqrt(total / C + EPSILON)
    inner = pltpu.roll(total, BLOCKS, 0) * scale / C
    both = jnp.where(line < BLOCKS, scale, pltpu.roll(inner, BLOCKS, 0))
    columns = jnp.concatenate([both] * 16, axis=0).T
    gain = small[21:22, :]
    gain_total = jnp.zeros((8, LANES), F32)
    for b in range(BLOCKS):
        here = slice(b * KM, (b + 1) * KM)
        scale_b = jnp.broadcast_to(columns[:, b : b + 1], (KM, LANES))
        inner_b = jnp.broadcast_to(columns[:, b + BLOCKS : b + BLOCKS + 1], (KM, LANES))
        query_feature = feature[0, here, :].astype(F32)
        answer = response[here, :]
        gated = (query_feature * answer).astype(BF16).astype(F32)
        normed = gated * scale_b
        out[here, :] = (normed * gain).astype(BF16)
        grad = out_grad[here, :].astype(F32)
        gain_total = gain_total + fold8(grad * normed)
        d_gated = (scale_b * (grad * gain - normed * inner_b)).astype(BF16).astype(F32)
        query[here, :] = (d_gated * answer).astype(BF16)
        reply[here, :] = (d_gated * query_feature).astype(BF16)
    gain_sum[...] = gain_total

    _, carry_next, _ = block_facts(records, tails, first)
    window[:KM, :] = reply[:KM, :].astype(F32)
    window[KM:, :] = reply[KM : KM + UNIT, :].astype(F32) * carry_next
    totals = [jnp.zeros((8, LANES), F32) for _ in range(4)]
    for lag in range(KM):
        totals[lag % 4] = totals[lag % 4] + mixer[lag : lag + 1, :] * window[lag : lag + 8, :]
    d_mixed = (totals[0] + totals[1]) + (totals[2] + totals[3])
    d_mixed = jnp.concatenate([d_mixed, jnp.zeros_like(d_mixed)], axis=0)
    rim[:KM, :] = reply[:KM, :]
    rim[KM : KM + UNIT, :] = query[:UNIT, :]
    rim[KM + UNIT : KM + 2 * UNIT, :] = (d_mixed * feature[2, :UNIT, :].astype(F32)).astype(BF16)
    rim[KM + 2 * UNIT :, :] = (d_mixed * feature[1, :UNIT, :].astype(F32)).astype(BF16)


def backward_kernel(
    slot,
    records,
    tails,
    position,
    query,
    reply,
    rim_back,
    feature,
    packed,
    rim,
    mixer,
    small,
    gain_sum,
    back,
    mixed,
    replies,
    pair,
    shifted,
    lag_total,
    d_feature,
    window,
    tap_total,
    spread,
):
    first = position[0] * BLOCKS
    mixed[:KM, :] = rim[:KM, :].astype(F32)
    replies[ROWS:, :] = rim_back[:KM, :].astype(F32)
    for b in range(BLOCKS):
        here = slice(b * KM, (b + 1) * KM)
        product = feature[1, here, :].astype(F32) * feature[2, here, :].astype(F32)
        mixed[(b + 1) * KM : (b + 2) * KM, :] = product.astype(BF16).astype(F32)
        replies[here, :] = reply[here, :].astype(F32)
    for s in range(3):
        d_feature[s, ROWS:, :] = rim_back[KM + s * UNIT : KM + (s + 1) * UNIT, :].astype(F32)
    d_feature[0, :ROWS, :] = query[...].astype(F32)
    lag_total[...] = jnp.zeros_like(lag_total)

    def one_block(b, unused):
        carry, carry_next, _ = block_facts(records, tails, first + b)
        here = pl.ds(pl.multiple_of(b * KM, KM), KM)
        after = pl.ds(pl.multiple_of((b + 1) * KM, KM), KM)
        pair[:KM, :] = replies[here, :]
        pair[KM:, :] = replies[after, :] * carry_next
        for s in range(8):
            shifted[s, : 2 * KM - 8, :] = pair[s : 2 * KM - 8 + s, :]
        total = jnp.zeros((KM, LANES), F32)
        for s in range(8):
            for k in range(16):
                lag = 8 * k + s
                total = total + mixer[lag : lag + 1, :] * shifted[s, 8 * k : 8 * k + KM, :]
        d_feature[1, here, :] = (total * feature[2, here, :].astype(F32)).astype(BF16).astype(F32)
        d_feature[2, here, :] = (total * feature[1, here, :].astype(F32)).astype(BF16).astype(F32)
        pair[:KM, :] = mixed[here, :] * carry
        pair[KM:, :] = mixed[after, :]
        for s in range(8):
            shifted[s, 8:, :] = pair[8 - s : 2 * KM - s, :]
        own = replies[here, :]
        for s in range(8):
            for k in range(16):
                lag = 8 * k + s
                lag_total[lag] = lag_total[lag] + fold8(
                    own * shifted[s, KM - 8 * k : 2 * KM - 8 * k, :]
                )
        return unused

    lax.fori_loop(0, BLOCKS, one_block, 0)

    tap_total[...] = jnp.zeros_like(tap_total)
    for b in range(BLOCKS):
        carry, carry_next, _ = block_facts(records, tails, first + b)
        here = slice(b * KM, (b + 1) * KM)
        for s in range(3):
            if b == 0:
                tail = rim[KM + s * UNIT : KM + (s + 1) * UNIT, :].astype(F32)
            else:
                tail = packed[s, b * KM - UNIT : b * KM, :].astype(F32)
            window[:UNIT, :] = tail * carry
            window[UNIT:, :] = packed[s, here, :].astype(F32)
            own = d_feature[s, here, :]
            for tap in range(KF):
                row = tap * 3 + s
                tap_total[row] = tap_total[row] + fold8(own * window[UNIT - tap : UNIT - tap + KM, :])
            window[:KM, :] = own
            window[KM:, :] = d_feature[s, (b + 1) * KM : (b + 1) * KM + UNIT, :] * carry_next
            total = jnp.zeros((KM, LANES), F32)
            for tap in range(KF):
                row = tap * 3 + s
                total = total + small[row : row + 1, :] * window[tap : tap + KM, :]
            spread[s, here, :] = total.astype(BF16)

    tap_total[21] = gain_sum[...]
    mixer_parts = parts_of(jnp.sum(lag_total[...], axis=1).T)
    small_parts = parts_of(jnp.sum(tap_total[...], axis=1))
    rest = jnp.zeros((KM - 96, LANES), F32)
    turned = jnp.concatenate(list(small_parts) + [rest], axis=0).T
    for shard in range(SHARDS):
        rows = slice(shard * 8, shard * 8 + 8)
        pieces = jnp.concatenate([part[rows] for part in mixer_parts] + [turned[rows]], axis=0)
        back[shard, 3 * CAP * UNIT :, :] = pieces.astype(BF16)

    def move(unit, carry):
        to = slot[unit]
        shard = to // CAP
        rank = to % CAP
        for s in range(3):
            back[shard, pl.ds(pl.multiple_of((s * CAP + rank) * UNIT, UNIT), UNIT), :] = spread[
                s, pl.ds(pl.multiple_of(unit * UNIT, UNIT), UNIT), :
            ]
        return carry

    lax.fori_loop(0, UNITS_DEV, move, 0)


def finish_kernel(slot, returned, stream_grad, grads):
    def move(unit, carry):
        at = slot[unit]
        shard = at // CAP
        rank = at % CAP
        for s in range(3):
            stream_grad[s, pl.ds(pl.multiple_of(unit * UNIT, UNIT), UNIT), :] = returned[
                shard, pl.ds(pl.multiple_of((s * CAP + rank) * UNIT, UNIT), UNIT), :
            ]
        return carry

    lax.fori_loop(0, UNITS_DEV, move, 0)
    total = jnp.zeros((2 * UNIT, LANES), F32)
    for shard in range(SHARDS):
        total = total + returned[shard, 3 * CAP * UNIT :, :].astype(F32)
    grads[:, :KM] = total[0:8] + total[8:16] + total[16:24]
    pieces = total[24:32]
    grads[:, KM:] = pieces + pltpu.roll(pieces, LANES - 32, 1) + pltpu.roll(pieces, LANES - 64, 1)

MESH = pl.DeviceIdType.MESH


def remote_call(kernel, out_shape, scratch, collective, *operands):
    return pl.pallas_call(
        kernel,
        out_shape=out_shape,
        in_specs=[VMEM] * len(operands),
        out_specs=VMEM,
        scratch_shapes=scratch,
        compiler_params=pltpu.CompilerParams(collective_id=collective, has_side_effects=True),
    )(*operands)


def exchange_kernel(blocks, out, sent, came, own):
    member = lax.axis_index("fsdp")
    me = lax.axis_index("seq")
    row, half = me // 2, me % 2
    peers = []
    for away in (1, 7, 2, 6, 3, 5, 4):
        peers.append((away, half))
        peers.append((away, 1 - half))
    peers.append((0, 1 - half))
    barrier = pltpu.get_barrier_semaphore()
    for away, side in peers:
        to = (row + away) % 8 * 2 + side
        pl.semaphore_signal(barrier, inc=1, device_id=(member, to), device_id_type=MESH)
    pl.semaphore_wait(barrier, len(peers))
    mine = pltpu.make_async_copy(blocks.at[me], out.at[me], own)
    mine.start()
    copies = []
    for number, (away, side) in enumerate(peers):
        to = (row + away) % 8 * 2 + side
        copy = pltpu.make_async_remote_copy(
            src_ref=blocks.at[to],
            dst_ref=out.at[me],
            send_sem=sent.at[number],
            recv_sem=came.at[number],
            device_id=(member, to),
            device_id_type=MESH,
        )
        copy.start()
        copies.append(copy)
    mine.wait()
    for copy in copies:
        copy.wait_send()
    for copy in copies:
        copy.wait_recv()


def exchange(blocks, collective):
    if INTERPRET:
        return lax.all_to_all(blocks, "seq", split_axis=0, concat_axis=0, tiled=True)
    return remote_call(
        exchange_kernel,
        shape(*blocks.shape, dtype=blocks.dtype),
        [
            pltpu.SemaphoreType.DMA((SHARDS,)),
            pltpu.SemaphoreType.DMA((SHARDS,)),
            pltpu.SemaphoreType.DMA,
        ],
        collective,
        blocks,
    )


def gather_kernel(value, out, sent, came, own):
    members = out.shape[0]
    member = lax.axis_index("fsdp")
    me = lax.axis_index("seq")
    barrier = pltpu.get_barrier_semaphore()
    for away in range(1, members):
        to = (member + away) % members
        pl.semaphore_signal(barrier, inc=1, device_id=(to, me), device_id_type=MESH)
    pl.semaphore_wait(barrier, members - 1)
    mine = pltpu.make_async_copy(value, out.at[member], own)
    mine.start()
    copies = []
    for away in range(1, members):
        to = (member + away) % members
        copy = pltpu.make_async_remote_copy(
            src_ref=value,
            dst_ref=out.at[member],
            send_sem=sent.at[away],
            recv_sem=came.at[away],
            device_id=(to, me),
            device_id_type=MESH,
        )
        copy.start()
        copies.append(copy)
    mine.wait()
    for copy in copies:
        copy.wait_send()
    for copy in copies:
        copy.wait_recv()


def gather(value, members, collective):
    if INTERPRET:
        return lax.all_gather(value, "fsdp")
    return remote_call(
        gather_kernel,
        shape(members, *value.shape, dtype=value.dtype),
        [
            pltpu.SemaphoreType.DMA((members,)),
            pltpu.SemaphoreType.DMA((members,)),
            pltpu.SemaphoreType.DMA,
        ],
        collective,
        value,
    )


def routing(unit_dest, position):
    target = (unit_dest // UNITS_DEV).reshape(SHARDS, UNITS_DEV)
    ids = jnp.arange(UNITS_DEV, dtype=jnp.int32)
    same = (target[:, :, None] == target[:, None, :]) & (ids[None, :] < ids[:, None])[None]
    rank = jnp.sum(same.astype(jnp.int32), axis=2)
    own_slot = lax.dynamic_index_in_dim(target * CAP + rank, position, 0, keepdims=False)
    arrive = (jnp.arange(SHARDS, dtype=jnp.int32)[:, None] * CAP + rank).reshape(-1)
    match = unit_dest[None, :] == (position * UNITS_DEV + ids)[:, None]
    packed_slot = jnp.sum(jnp.where(match, arrive[None, :], 0), axis=1)
    return own_slot.astype(jnp.int32), packed_slot.astype(jnp.int32)


def body(
    streams, record_blocks, tail_rows, unit_dest, mixer_filter, feat_filter, norm_gain, out_grad
):
    members = lax.axis_size("fsdp")
    position = lax.axis_index("seq").astype(jnp.int32)
    own_slot, packed_slot = routing(unit_dest, position)
    where = position.reshape(1)
    filters = jnp.concatenate(
        [
            mixer_filter,
            feat_filter.reshape(KF * 3, 8),
            norm_gain.reshape(1, 8),
            jnp.zeros((LANES - KF * 3 - 1, 8), F32),
        ],
        axis=0,
    ).T
    outgoing = call(
        pack_kernel,
        shape(SHARDS, OUT_UNITS * UNIT, LANES),
        [],
        own_slot,
        streams,
        filters,
        scalars=1,
    )
    arrived = exchange(outgoing, 0)
    facts = (record_blocks, tail_rows, where)
    packed, mixer, small, rim_out = call(
        unpack_kernel,
        (
            shape(3, ROWS, LANES),
            shape(KM, LANES, dtype=F32),
            shape(32, LANES, dtype=F32),
            shape(RIM, LANES),
        ),
        [pltpu.VMEM((2, LANES, LANES), F32)],
        packed_slot,
        *facts,
        arrived,
        scalars=4,
    )
    rim = lax.ppermute(rim_out, "seq", [(i, i + 1) for i in range(SHARDS - 1)])
    feature, response, sums = call(
        forward_kernel,
        (
            shape(3, ROWS, LANES),
            shape(ROWS, LANES, dtype=F32),
            shape(8, LANES, dtype=F32),
        ),
        [
            pltpu.VMEM((3, UNIT + KM, LANES), F32),
            pltpu.VMEM((ROWS + KM, LANES), F32),
            pltpu.VMEM((2 * KM, LANES), F32),
            pltpu.VMEM((8, 2 * KM, LANES), F32),
        ],
        *facts,
        packed,
        rim,
        mixer,
        small,
        out_grad,
        scalars=3,
    )
    sums = gather(sums, members, 1)
    out, query, reply, gain_sum, rim_back_out = call(
        middle_kernel,
        (
            shape(ROWS, LANES),
            shape(ROWS, LANES),
            shape(ROWS, LANES),
            shape(8, LANES, dtype=F32),
            shape(RIM, LANES),
        ),
        [pltpu.VMEM((KM + UNIT, LANES), F32)],
        *facts,
        sums,
        feature,
        response,
        mixer,
        small,
        out_grad,
        scalars=3,
    )
    rim_back = lax.ppermute(rim_back_out, "seq", [(i + 1, i) for i in range(SHARDS - 1)])
    returning = call(
        backward_kernel,
        shape(SHARDS, BACK_UNITS * UNIT, LANES),
        [
            pltpu.VMEM((ROWS + KM, LANES), F32),
            pltpu.VMEM((ROWS + KM, LANES), F32),
            pltpu.VMEM((2 * KM, LANES), F32),
            pltpu.VMEM((8, 2 * KM, LANES), F32),
            pltpu.VMEM((KM, 8, LANES), F32),
            pltpu.VMEM((3, ROWS + UNIT, LANES), F32),
            pltpu.VMEM((KM + UNIT, LANES), F32),
            pltpu.VMEM((32, 8, LANES), F32),
            pltpu.VMEM((3, ROWS, LANES), BF16),
        ],
        packed_slot,
        *facts,
        query,
        reply,
        rim_back,
        feature,
        packed,
        rim,
        mixer,
        small,
        gain_sum,
        scalars=4,
    )
    returned = exchange(returning, 2)
    stream_grad, grads = call(
        finish_kernel,
        (shape(3, ROWS, LANES), shape(8, 2 * LANES, dtype=F32)),
        [],
        own_slot,
        returned,
        scalars=1,
    )
    turned = grads.T
    mixer_grad = turned[:KM]
    feat_grad = turned[KM : KM + KF * 3].reshape(KF, 3, 8)
    gain_grad = turned[KM + KF * 3]
    return (out, stream_grad, mixer_grad, feat_grad, gain_grad)


def solution(mesh):
    placed = (
        P(None, "seq", "fsdp"),
        P(),
        P(),
        P(),
        P(None, ("fsdp", "seq")),
        P(None, None, ("fsdp", "seq")),
        P(("fsdp", "seq")),
        P("seq", "fsdp"),
    )
    return jax.shard_map(
        body,
        mesh=mesh,
        in_specs=placed,
        out_specs=(
            P("seq", "fsdp"),
            P(None, "seq", "fsdp"),
            P(None, ("fsdp", "seq")),
            P(None, None, ("fsdp", "seq")),
            P(("fsdp", "seq")),
        ),
        check_vma=False,
    )
```

```python
import functools

import jax
import jax.numpy as jnp
from jax import lax
from jax.experimental import pallas as pl
from jax.experimental.pallas import tpu as pltpu
from jax.sharding import PartitionSpec as P

C = 4096
KM = 128
KF = 7
UNIT = 16
CAP = 4
EPSILON = 1e-06
INTERPRET = False

F32 = jnp.float32
BF16 = jnp.bfloat16
VMEM = pl.BlockSpec(memory_space=pltpu.VMEM)
SMEM = pl.BlockSpec(memory_space=pltpu.SMEM)

LANES = 128
BLOCKS = 4
ROWS = BLOCKS * KM
SHARDS = 16
UNITS_DEV = ROWS // UNIT
OUT_UNITS = 3 * CAP + 1
BACK_UNITS = 3 * CAP + 2
RIM = KM + 3 * UNIT


def call(kernel, out_shape, scratch, *operands, scalars=0):
    return pl.pallas_call(
        kernel,
        out_shape=out_shape,
        in_specs=[SMEM] * scalars + [VMEM] * (len(operands) - scalars),
        out_specs=jax.tree.map(lambda _: VMEM, out_shape),
        scratch_shapes=scratch,
        interpret=INTERPRET,
    )(*operands)


def shape(*dims, dtype=BF16):
    return jax.ShapeDtypeStruct(dims, dtype)


def parts_of(value):
    high = value.astype(BF16).astype(F32)
    rest = value - high
    middle = rest.astype(BF16).astype(F32)
    return high, middle, rest - middle


def block_facts(records, tails, block):
    second = records[0]
    third = records[0] + records[1]
    end = third + records[2]

    def begins(index):
        return (index == 0) | (index == second) | (index == third)

    used = jnp.where(
        block + 1 == second,
        tails[0],
        jnp.where(block + 1 == third, tails[1], jnp.where(block + 1 == end, tails[2], KM)),
    )
    carry = jnp.where(begins(block), 0.0, 1.0).astype(F32)
    carry_next = jnp.where(begins(block + 1) | (block + 1 == end), 0.0, 1.0).astype(F32)
    return carry, carry_next, used


def write_facts(facts, records, tails, first):
    line = lax.broadcasted_iota(jnp.int32, (16, LANES), 0)
    rows = jnp.zeros((16, LANES), F32)
    for b in range(BLOCKS):
        carry, carry_next, used = block_facts(records, tails, first + b)
        rows = jnp.where(line == b, carry, rows)
        rows = jnp.where(line == b + BLOCKS, carry_next, rows)
        rows = jnp.where(line == b + 2 * BLOCKS, used.astype(F32), rows)
    facts[...] = rows


def carry_of(facts, b):
    return facts[pl.ds(b, 1), :]


def carry_next_of(facts, b):
    return facts[pl.ds(b + BLOCKS, 1), :]


def live_of(facts, b):
    rows = lax.broadcasted_iota(jnp.int32, (KM, LANES), 0).astype(F32)
    return jnp.where(rows < facts[pl.ds(b + 2 * BLOCKS, 1), :], 1.0, 0.0)


def fold8(value):
    return jnp.sum(value.reshape(-1, 8, LANES), axis=0)


def pack_kernel(slot, records, tails, position, streams, filters, out, facts):
    write_facts(facts, records, tails, position[0] * BLOCKS)
    taps = filters[...]
    high, middle, low = parts_of(taps[:, KM:])
    lane = lax.broadcasted_iota(jnp.int32, (8, LANES), 1)
    small = jnp.where(
        lane < 32,
        high,
        jnp.where(
            lane < 64,
            pltpu.roll(middle, 32, 1),
            jnp.where(lane < 96, pltpu.roll(low, 64, 1), 0.0),
        ),
    )
    panel = jnp.concatenate([taps[:, :KM], small], axis=0).astype(BF16)

    def give(shard, carry):
        out[shard, pl.ds(3 * CAP * UNIT, UNIT), :] = panel
        return carry

    lax.fori_loop(0, SHARDS, give, 0)

    def move(unit, carry):
        to = slot[unit]
        shard = to // CAP
        rank = to % CAP
        for s in range(3):
            out[shard, pl.ds(pl.multiple_of((s * CAP + rank) * UNIT, UNIT), UNIT), :] = streams[
                s, pl.ds(pl.multiple_of(unit * UNIT, UNIT), UNIT), :
            ]
        return carry

    lax.fori_loop(0, UNITS_DEV, move, 0)


def unpack_kernel(slot, facts, arrived, packed, mixer, small, rim, turned):
    def move(unit, carry):
        at = slot[unit]
        shard = at // CAP
        rank = at % CAP
        for s in range(3):
            packed[s, pl.ds(pl.multiple_of(unit * UNIT, UNIT), UNIT), :] = arrived[
                shard, pl.ds(pl.multiple_of((s * CAP + rank) * UNIT, UNIT), UNIT), :
            ]
        return carry

    lax.fori_loop(0, UNITS_DEV, move, 0)
    for shard in range(SHARDS):
        panel = arrived[shard, 3 * CAP * UNIT :, :].astype(F32)
        turned[0, shard * 8 : shard * 8 + 8, :] = panel[:8]
        turned[1, shard * 8 : shard * 8 + 8, :] = panel[8:]
    mixer[...] = turned[0].T
    pieces = turned[1].T
    small[...] = pieces[0:32] + pieces[32:64] + pieces[64:96]

    carry = carry_of(facts, BLOCKS - 1)
    live = live_of(facts, BLOCKS - 1)
    heads = lax.broadcasted_iota(jnp.int32, (KM + UNIT, LANES), 0) < UNIT
    keep = jnp.where(heads, carry, 1.0)
    both = []
    for s in (1, 2):
        wide = packed[s, ROWS - KM - UNIT :, :].astype(F32) * keep
        total = jnp.zeros((KM, LANES), F32)
        for tap in range(KF):
            row = tap * 3 + s
            total = total + small[row : row + 1, :] * wide[UNIT - tap : UNIT - tap + KM]
        both.append((total * live).astype(BF16).astype(F32))
    rim[:KM, :] = (both[0] * both[1]).astype(BF16)
    for s in range(3):
        rim[KM + s * UNIT : KM + (s + 1) * UNIT, :] = packed[s, ROWS - UNIT :, :]


def forward_kernel(
    facts,
    packed,
    rim,
    mixer,
    small,
    out_grad,
    feature,
    response,
    sums,
    window,
    mixed,
    pair,
    shifted,
):
    mixed[:KM, :] = rim[:KM, :].astype(F32)
    for b in range(BLOCKS):
        carry = carry_of(facts, b)
        live = live_of(facts, b)
        both = []
        for s in range(3):
            if b == 0:
                tail = rim[KM + s * UNIT : KM + (s + 1) * UNIT, :].astype(F32)
            else:
                tail = packed[s, b * KM - UNIT : b * KM, :].astype(F32)
            window[s, :UNIT, :] = tail * carry
            window[s, UNIT:, :] = packed[s, b * KM : (b + 1) * KM, :].astype(F32)
            total = jnp.zeros((KM, LANES), F32)
            for tap in range(KF):
                row = tap * 3 + s
                total = total + small[row : row + 1, :] * window[s, UNIT - tap : UNIT - tap + KM, :]
            rounded = (total * live).astype(BF16)
            feature[s, b * KM : (b + 1) * KM, :] = rounded
            both.append(rounded.astype(F32))
        mixed[(b + 1) * KM : (b + 2) * KM, :] = (both[1] * both[2]).astype(BF16).astype(F32)

    gain = small[21:22, :]
    ones = jnp.ones((8, LANES), F32)
    line = lax.broadcasted_iota(jnp.int32, (8, LANES), 0)

    def one_block(b, collected):
        carry = carry_of(facts, b)
        here = pl.ds(pl.multiple_of(b * KM, KM), KM)
        pair[:KM, :] = mixed[here, :] * carry
        pair[KM:, :] = mixed[pl.ds(pl.multiple_of((b + 1) * KM, KM), KM), :]
        for s in range(8):
            shifted[s, 8:, :] = pair[8 - s : 2 * KM - s, :]
        total = jnp.zeros((KM, LANES), F32)
        for s in range(8):
            for k in range(16):
                lag = 8 * k + s
                total = total + mixer[lag : lag + 1, :] * shifted[s, KM - 8 * k : 2 * KM - 8 * k, :]
        response[here, :] = total
        gated = (feature[0, here, :].astype(F32) * total).astype(BF16).astype(F32)
        weighted = out_grad[here, :].astype(F32) * gain
        contract = (((1,), (1,)), ((), ()))
        squares = lax.dot_general(
            ones, gated * gated, contract, precision=lax.Precision.HIGHEST,
            preferred_element_type=F32,
        )
        inner = lax.dot_general(
            ones, weighted * gated, contract, precision=lax.Precision.HIGHEST,
            preferred_element_type=F32,
        )
        return jnp.where(line == b, squares, jnp.where(line == b + BLOCKS, inner, collected))

    collected = lax.fori_loop(0, BLOCKS, one_block, jnp.zeros((8, LANES), F32))
    sums[...] = collected


def middle_kernel(
    facts,
    sums,
    feature,
    response,
    mixer,
    small,
    out_grad,
    out,
    query,
    reply,
    gain_sum,
    rim,
    window,
):
    total = jnp.sum(sums[...], axis=0)
    line = lax.broadcasted_iota(jnp.int32, (8, LANES), 0)
    lane = lax.broadcasted_iota(jnp.int32, (8, LANES), 1)
    used = facts[2 * BLOCKS :, :]
    scale = jnp.where(lane.astype(F32) < used, 1.0, 0.0) * lax.rsqrt(total / C + EPSILON)
    inner = pltpu.roll(total, BLOCKS, 0) * scale / C
    both = jnp.where(line < BLOCKS, scale, pltpu.roll(inner, BLOCKS, 0))
    columns = jnp.concatenate([both] * 16, axis=0).T
    gain = small[21:22, :]
    gain_total = jnp.zeros((8, LANES), F32)
    for b in range(BLOCKS):
        here = slice(b * KM, (b + 1) * KM)
        scale_b = jnp.broadcast_to(columns[:, b : b + 1], (KM, LANES))
        inner_b = jnp.broadcast_to(columns[:, b + BLOCKS : b + BLOCKS + 1], (KM, LANES))
        query_feature = feature[0, here, :].astype(F32)
        answer = response[here, :]
        gated = (query_feature * answer).astype(BF16).astype(F32)
        normed = gated * scale_b
        out[here, :] = (normed * gain).astype(BF16)
        grad = out_grad[here, :].astype(F32)
        gain_total = gain_total + fold8(grad * normed)
        d_gated = (scale_b * (grad * gain - normed * inner_b)).astype(BF16).astype(F32)
        query[here, :] = (d_gated * answer).astype(BF16)
        reply[here, :] = (d_gated * query_feature).astype(BF16)
    gain_sum[...] = gain_total

    carry_next = carry_next_of(facts, 0)
    window[:KM, :] = reply[:KM, :].astype(F32)
    window[KM:, :] = reply[KM : KM + UNIT, :].astype(F32) * carry_next
    totals = [jnp.zeros((8, LANES), F32) for _ in range(4)]
    for lag in range(KM):
        totals[lag % 4] = totals[lag % 4] + mixer[lag : lag + 1, :] * window[lag : lag + 8, :]
    d_mixed = (totals[0] + totals[1]) + (totals[2] + totals[3])
    d_mixed = jnp.concatenate([d_mixed, jnp.zeros_like(d_mixed)], axis=0)
    rim[:KM, :] = reply[:KM, :]
    rim[KM : KM + UNIT, :] = query[:UNIT, :]
    rim[KM + UNIT : KM + 2 * UNIT, :] = (d_mixed * feature[2, :UNIT, :].astype(F32)).astype(BF16)
    rim[KM + 2 * UNIT :, :] = (d_mixed * feature[1, :UNIT, :].astype(F32)).astype(BF16)


def backward_kernel(
    source,
    facts,
    query,
    reply,
    rim_back,
    feature,
    packed,
    rim,
    mixer,
    small,
    gain_sum,
    back,
    mixed,
    replies,
    pair,
    shifted,
    lag_total,
    d_feature,
    window,
    tap_total,
    spread,
):
    mixed[:KM, :] = rim[:KM, :].astype(F32)
    replies[ROWS:, :] = rim_back[:KM, :].astype(F32)
    for b in range(BLOCKS):
        here = slice(b * KM, (b + 1) * KM)
        product = feature[1, here, :].astype(F32) * feature[2, here, :].astype(F32)
        mixed[(b + 1) * KM : (b + 2) * KM, :] = product.astype(BF16).astype(F32)
        replies[here, :] = reply[here, :].astype(F32)
    for s in range(3):
        d_feature[s, ROWS:, :] = rim_back[KM + s * UNIT : KM + (s + 1) * UNIT, :].astype(F32)
    d_feature[0, :ROWS, :] = query[...].astype(F32)
    lag_total[...] = jnp.zeros_like(lag_total)

    def one_block(b, unused):
        carry, carry_next = carry_of(facts, b), carry_next_of(facts, b)
        here = pl.ds(pl.multiple_of(b * KM, KM), KM)
        after = pl.ds(pl.multiple_of((b + 1) * KM, KM), KM)
        pair[:KM, :] = replies[here, :]
        pair[KM:, :] = replies[after, :] * carry_next
        for s in range(8):
            shifted[s, : 2 * KM - 8, :] = pair[s : 2 * KM - 8 + s, :]
        total = jnp.zeros((KM, LANES), F32)
        for s in range(8):
            for k in range(16):
                lag = 8 * k + s
                total = total + mixer[lag : lag + 1, :] * shifted[s, 8 * k : 8 * k + KM, :]
        d_feature[1, here, :] = (total * feature[2, here, :].astype(F32)).astype(BF16).astype(F32)
        d_feature[2, here, :] = (total * feature[1, here, :].astype(F32)).astype(BF16).astype(F32)
        pair[:KM, :] = mixed[here, :] * carry
        pair[KM:, :] = mixed[after, :]
        for s in range(8):
            shifted[s, 8:, :] = pair[8 - s : 2 * KM - s, :]
        own = replies[here, :]
        for s in range(8):
            for k in range(16):
                lag = 8 * k + s
                lag_total[lag] = lag_total[lag] + fold8(
                    own * shifted[s, KM - 8 * k : 2 * KM - 8 * k, :]
                )
        return unused

    lax.fori_loop(0, BLOCKS, one_block, 0)

    tap_total[...] = jnp.zeros_like(tap_total)
    for b in range(BLOCKS):
        carry, carry_next = carry_of(facts, b), carry_next_of(facts, b)
        here = slice(b * KM, (b + 1) * KM)
        for s in range(3):
            if b == 0:
                tail = rim[KM + s * UNIT : KM + (s + 1) * UNIT, :].astype(F32)
            else:
                tail = packed[s, b * KM - UNIT : b * KM, :].astype(F32)
            window[:UNIT, :] = tail * carry
            window[UNIT:, :] = packed[s, here, :].astype(F32)
            own = d_feature[s, here, :]
            for tap in range(KF):
                row = tap * 3 + s
                tap_total[row] = tap_total[row] + fold8(own * window[UNIT - tap : UNIT - tap + KM, :])
            window[:KM, :] = own
            window[KM:, :] = d_feature[s, (b + 1) * KM : (b + 1) * KM + UNIT, :] * carry_next
            total = jnp.zeros((KM, LANES), F32)
            for tap in range(KF):
                row = tap * 3 + s
                total = total + small[row : row + 1, :] * window[tap : tap + KM, :]
            spread[s, here, :] = total.astype(BF16)

    tap_total[21] = gain_sum[...]
    mixer_parts = parts_of(jnp.sum(lag_total[...], axis=1).T)
    small_parts = parts_of(jnp.sum(tap_total[...], axis=1))
    rest = jnp.zeros((KM - 96, LANES), F32)
    turned = jnp.concatenate(list(small_parts) + [rest], axis=0).T
    for shard in range(SHARDS):
        rows = slice(shard * 8, shard * 8 + 8)
        pieces = jnp.concatenate([part[rows] for part in mixer_parts] + [turned[rows]], axis=0)
        back[shard, 3 * CAP * UNIT :, :] = pieces.astype(BF16)

    def move(place, carry):
        unit = source[place]
        shard = place // CAP
        rank = place % CAP
        for s in range(3):
            back[shard, pl.ds(pl.multiple_of((s * CAP + rank) * UNIT, UNIT), UNIT), :] = spread[
                s, pl.ds(pl.multiple_of(unit * UNIT, UNIT), UNIT), :
            ]
        return carry

    lax.fori_loop(0, SHARDS * CAP, move, 0)


def finish_kernel(slot, returned, stream_grad, grads):
    def move(unit, carry):
        at = slot[unit]
        shard = at // CAP
        rank = at % CAP
        for s in range(3):
            stream_grad[s, pl.ds(pl.multiple_of(unit * UNIT, UNIT), UNIT), :] = returned[
                shard, pl.ds(pl.multiple_of((s * CAP + rank) * UNIT, UNIT), UNIT), :
            ]
        return carry

    lax.fori_loop(0, UNITS_DEV, move, 0)
    total = jnp.zeros((2 * UNIT, LANES), F32)
    for shard in range(SHARDS):
        total = total + returned[shard, 3 * CAP * UNIT :, :].astype(F32)
    grads[:, :KM] = total[0:8] + total[8:16] + total[16:24]
    pieces = total[24:32]
    grads[:, KM:] = pieces + pltpu.roll(pieces, LANES - 32, 1) + pltpu.roll(pieces, LANES - 64, 1)

MESH = pl.DeviceIdType.MESH


def remote_call(kernel, out_shape, scratch, collective, *operands, scalars=0):
    return pl.pallas_call(
        kernel,
        out_shape=out_shape,
        in_specs=[SMEM] * scalars + [VMEM] * (len(operands) - scalars),
        out_specs=jax.tree.map(lambda _: VMEM, out_shape),
        scratch_shapes=scratch,
        compiler_params=pltpu.CompilerParams(collective_id=collective, has_side_effects=True),
    )(*operands)


def shard_peers():
    member = lax.axis_index("fsdp")
    me = lax.axis_index("seq")
    row, half = me // 2, me % 2
    peers = []
    for away in (1, 7, 2, 6, 3, 5, 4):
        peers.append((row + away) % 8 * 2 + half)
        peers.append((row + away) % 8 * 2 + 1 - half)
    peers.append(row * 2 + 1 - half)
    return member, me, peers


def greet(devices):
    barrier = pltpu.get_barrier_semaphore()
    for device in devices:
        pl.semaphore_signal(barrier, inc=1, device_id=device, device_id_type=MESH)


def met(count):
    pl.semaphore_wait(pltpu.get_barrier_semaphore(), count)


def finish_copies(copies):
    for copy in copies:
        copy.wait_send()
    for copy in copies:
        copy.wait_recv()


def deal(blocks, out, sent, came, own):
    member, me, peers = shard_peers()
    mine = pltpu.make_async_copy(blocks.at[me], out.at[me], own)
    mine.start()
    copies = []
    for number, to in enumerate(peers):
        copy = pltpu.make_async_remote_copy(
            src_ref=blocks.at[to],
            dst_ref=out.at[me],
            send_sem=sent.at[number],
            recv_sem=came.at[number],
            device_id=(member, to),
            device_id_type=MESH,
        )
        copy.start()
        copies.append(copy)
    mine.wait()
    finish_copies(copies)


def pass_on(source, target, sent, came, by):
    member = lax.axis_index("fsdp")
    to = lax.rem(lax.axis_index("seq") + SHARDS + by, SHARDS)
    copy = pltpu.make_async_remote_copy(
        src_ref=source,
        dst_ref=target,
        send_sem=sent,
        recv_sem=came,
        device_id=(member, to),
        device_id_type=MESH,
    )
    copy.start()
    copy.wait()


def exchange_kernel(blocks, out, sent, came, own):
    member, _, peers = shard_peers()
    greet([(member, to) for to in peers])
    met(len(peers))
    deal(blocks, out, sent, came, own)


def middle_remote_kernel(
    facts, packed, rim, mixer, small, out_grad,
    feature, out, query, reply, gain_sum, rim_back,
    response, collected, sums, rim_out, window3, mixed, pair, shifted, window,
    sent, came, own, rim_sent, rim_came,
):
    members = sums.shape[0]
    member = lax.axis_index("fsdp")
    me = lax.axis_index("seq")
    others = [(lax.rem(member + away, members), me) for away in range(1, members)]
    greet(others + [(member, lax.rem(me + 1, SHARDS))])
    forward_kernel(
        facts, packed, rim, mixer, small, out_grad,
        feature, response, collected, window3, mixed, pair, shifted,
    )
    met(members)
    mine = pltpu.make_async_copy(collected, sums.at[member], own)
    mine.start()
    copies = []
    for number, device in enumerate(others):
        copy = pltpu.make_async_remote_copy(
            src_ref=collected,
            dst_ref=sums.at[member],
            send_sem=sent.at[number],
            recv_sem=came.at[number],
            device_id=device,
            device_id_type=MESH,
        )
        copy.start()
        copies.append(copy)
    mine.wait()
    finish_copies(copies)
    middle_kernel(
        facts, sums, feature, response, mixer, small, out_grad,
        out, query, reply, gain_sum, rim_out, window,
    )
    pass_on(rim_out, rim_back, rim_sent, rim_came, -1)


def exchange(blocks, collective):
    if INTERPRET:
        return lax.all_to_all(blocks, "seq", split_axis=0, concat_axis=0, tiled=True)
    return remote_call(
        exchange_kernel,
        shape(*blocks.shape, dtype=blocks.dtype),
        [
            pltpu.SemaphoreType.DMA((SHARDS,)),
            pltpu.SemaphoreType.DMA((SHARDS,)),
            pltpu.SemaphoreType.DMA,
        ],
        collective,
        blocks,
    )


def routing(unit_dest, position):
    target = (unit_dest // UNITS_DEV).reshape(SHARDS, UNITS_DEV)
    ids = jnp.arange(UNITS_DEV, dtype=jnp.int32)
    same = (target[:, :, None] == target[:, None, :]) & (ids[None, :] < ids[:, None])[None]
    rank = jnp.sum(same.astype(jnp.int32), axis=2)
    own_slot = lax.dynamic_index_in_dim(target * CAP + rank, position, 0, keepdims=False)
    arrive = (jnp.arange(SHARDS, dtype=jnp.int32)[:, None] * CAP + rank).reshape(-1)
    match = unit_dest[None, :] == (position * UNITS_DEV + ids)[:, None]
    packed_slot = jnp.sum(jnp.where(match, arrive[None, :], 0), axis=1)
    places = jnp.arange(SHARDS * CAP, dtype=jnp.int32)[:, None]
    back_source = jnp.sum(jnp.where(packed_slot[None, :] == places, ids[None, :], 0), axis=1)
    return own_slot, packed_slot, back_source


def body(
    streams, record_blocks, tail_rows, unit_dest, mixer_filter, feat_filter, norm_gain, out_grad
):
    members = lax.axis_size("fsdp")
    position = lax.axis_index("seq").astype(jnp.int32)
    own_slot, packed_slot, back_source = routing(unit_dest, position)
    where = position.reshape(1)
    filters = jnp.concatenate(
        [
            mixer_filter,
            feat_filter.reshape(KF * 3, 8),
            norm_gain.reshape(1, 8),
            jnp.zeros((LANES - KF * 3 - 1, 8), F32),
        ],
        axis=0,
    ).T
    outgoing, facts = call(
        pack_kernel,
        (shape(SHARDS, OUT_UNITS * UNIT, LANES), shape(16, LANES, dtype=F32)),
        [],
        own_slot,
        record_blocks,
        tail_rows,
        where,
        streams,
        filters,
        scalars=4,
    )
    arrived = exchange(outgoing, 0)
    packed, mixer, small, rim_out = call(
        unpack_kernel,
        (
            shape(3, ROWS, LANES),
            shape(KM, LANES, dtype=F32),
            shape(32, LANES, dtype=F32),
            shape(RIM, LANES),
        ),
        [pltpu.VMEM((2, LANES, LANES), F32)],
        packed_slot,
        facts,
        arrived,
        scalars=1,
    )
    rim = lax.ppermute(rim_out, "seq", [(i, i + 1) for i in range(SHARDS - 1)])
    feature, out, query, reply, gain_sum, rim_back = remote_call(
        middle_remote_kernel,
        (
            shape(3, ROWS, LANES),
            shape(ROWS, LANES),
            shape(ROWS, LANES),
            shape(ROWS, LANES),
            shape(8, LANES, dtype=F32),
            shape(RIM, LANES),
        ),
        [
            pltpu.VMEM((ROWS, LANES), F32),
            pltpu.VMEM((8, LANES), F32),
            pltpu.VMEM((members, 8, LANES), F32),
            pltpu.VMEM((RIM, LANES), BF16),
            pltpu.VMEM((3, UNIT + KM, LANES), F32),
            pltpu.VMEM((ROWS + KM, LANES), F32),
            pltpu.VMEM((2 * KM, LANES), F32),
            pltpu.VMEM((8, 2 * KM, LANES), F32),
            pltpu.VMEM((KM + UNIT, LANES), F32),
            pltpu.SemaphoreType.DMA((members,)),
            pltpu.SemaphoreType.DMA((members,)),
            pltpu.SemaphoreType.DMA,
            pltpu.SemaphoreType.DMA,
            pltpu.SemaphoreType.DMA,
        ],
        1,
        facts,
        packed,
        rim,
        mixer,
        small,
        out_grad,
    )
    returning = call(
        backward_kernel,
        shape(SHARDS, BACK_UNITS * UNIT, LANES),
        [
            pltpu.VMEM((ROWS + KM, LANES), F32),
            pltpu.VMEM((ROWS + KM, LANES), F32),
            pltpu.VMEM((2 * KM, LANES), F32),
            pltpu.VMEM((8, 2 * KM, LANES), F32),
            pltpu.VMEM((KM, 8, LANES), F32),
            pltpu.VMEM((3, ROWS + UNIT, LANES), F32),
            pltpu.VMEM((KM + UNIT, LANES), F32),
            pltpu.VMEM((32, 8, LANES), F32),
            pltpu.VMEM((3, ROWS, LANES), BF16),
        ],
        back_source,
        facts,
        query,
        reply,
        rim_back,
        feature,
        packed,
        rim,
        mixer,
        small,
        gain_sum,
        scalars=1,
    )
    returned = exchange(returning, 2)
    stream_grad, grads = call(
        finish_kernel,
        (shape(3, ROWS, LANES), shape(8, 2 * LANES, dtype=F32)),
        [],
        own_slot,
        returned,
        scalars=1,
    )
    turned = grads.T
    mixer_grad = turned[:KM]
    feat_grad = turned[KM : KM + KF * 3].reshape(KF, 3, 8)
    gain_grad = turned[KM + KF * 3]
    return (out, stream_grad, mixer_grad, feat_grad, gain_grad)


def solution(mesh):
    placed = (
        P(None, "seq", "fsdp"),
        P(),
        P(),
        P(),
        P(None, ("fsdp", "seq")),
        P(None, None, ("fsdp", "seq")),
        P(("fsdp", "seq")),
        P("seq", "fsdp"),
    )
    return jax.shard_map(
        body,
        mesh=mesh,
        in_specs=placed,
        out_specs=(
            P("seq", "fsdp"),
            P(None, "seq", "fsdp"),
            P(None, ("fsdp", "seq")),
            P(None, None, ("fsdp", "seq")),
            P(("fsdp", "seq")),
        ),
        check_vma=False,
    )
```

```python
import functools

import jax
import jax.numpy as jnp
from jax import lax
from jax.experimental import pallas as pl
from jax.experimental.pallas import tpu as pltpu
from jax.sharding import PartitionSpec as P

C = 4096
KM = 128
KF = 7
UNIT = 16
CAP = 4
EPSILON = 1e-06
INTERPRET = False

F32 = jnp.float32
BF16 = jnp.bfloat16
VMEM = pl.BlockSpec(memory_space=pltpu.VMEM)
SMEM = pl.BlockSpec(memory_space=pltpu.SMEM)

LANES = 128
BLOCKS = 4
ROWS = BLOCKS * KM
SHARDS = 16
UNITS_DEV = ROWS // UNIT
OUT_UNITS = 3 * CAP + 1
BACK_UNITS = 3 * CAP + 2
RIM = KM + 3 * UNIT
FROM_PACKED = 16
FROM_OWN = FROM_PACKED + UNITS_DEV
FROM_BACK = FROM_OWN + UNITS_DEV
FACTS = FROM_BACK + SHARDS * CAP
SLOT_ROWS = SHARDS * CAP * UNIT


def call(kernel, out_shape, scratch, *operands, scalars=0):
    return pl.pallas_call(
        kernel,
        out_shape=out_shape,
        in_specs=[SMEM] * scalars + [VMEM] * (len(operands) - scalars),
        out_specs=jax.tree.map(lambda _: VMEM, out_shape),
        scratch_shapes=scratch,
        interpret=INTERPRET,
    )(*operands)


def shape(*dims, dtype=BF16):
    return jax.ShapeDtypeStruct(dims, dtype)


def parts_of(value):
    high = value.astype(BF16).astype(F32)
    rest = value - high
    middle = rest.astype(BF16).astype(F32)
    return high, middle, rest - middle


def block_facts(records, tails, block):
    second = records[0]
    third = records[0] + records[1]
    end = third + records[2]

    def begins(index):
        return (index == 0) | (index == second) | (index == third)

    used = jnp.where(
        block + 1 == second,
        tails[0],
        jnp.where(block + 1 == third, tails[1], jnp.where(block + 1 == end, tails[2], KM)),
    )
    carry = jnp.where(begins(block), 0.0, 1.0).astype(F32)
    carry_next = jnp.where(begins(block + 1) | (block + 1 == end), 0.0, 1.0).astype(F32)
    return carry, carry_next, used


def write_facts(facts, records, tails, first):
    line = lax.broadcasted_iota(jnp.int32, (16, LANES), 0)
    rows = jnp.zeros((16, LANES), F32)
    for b in range(BLOCKS):
        carry, carry_next, used = block_facts(records, tails, first + b)
        rows = jnp.where(line == b, carry, rows)
        rows = jnp.where(line == b + BLOCKS, carry_next, rows)
        rows = jnp.where(line == b + 2 * BLOCKS, used.astype(F32), rows)
    facts[:16, :] = rows


def carry_of(facts, b):
    return facts[pl.ds(b, 1), :]


def carry_next_of(facts, b):
    return facts[pl.ds(b + BLOCKS, 1), :]


def live_of(facts, b):
    rows = lax.broadcasted_iota(jnp.int32, (KM, LANES), 0).astype(F32)
    return jnp.where(rows < facts[pl.ds(b + 2 * BLOCKS, 1), :], 1.0, 0.0)


def one_hot(matrix, facts, base):
    lanes = lax.broadcasted_iota(jnp.int32, (UNIT, LANES), 1)
    rows = lax.broadcasted_iota(jnp.int32, (UNIT, LANES), 0)
    offset = (lanes - rows).astype(F32)

    def unit_rows(unit, carry):
        start = facts[pl.ds(base + unit, 1), :]
        at = pl.ds(pl.multiple_of(unit * UNIT, UNIT), UNIT)
        for column in range(0, matrix.shape[1], LANES):
            picked = jnp.where(offset + column == start, 1.0, 0.0)
            matrix[at, column : column + LANES] = picked.astype(BF16)
        return carry

    lax.fori_loop(0, matrix.shape[0] // UNIT, unit_rows, 0)


def pick(matrix, table):
    return jnp.dot(matrix, table, preferred_element_type=F32).astype(BF16)


def slots_of(arrived, s):
    part = arrived[:, s * CAP * UNIT : (s + 1) * CAP * UNIT, :]
    return part.reshape(SLOT_ROWS, LANES)


def fold8(value):
    return jnp.sum(value.reshape(-1, 8, LANES), axis=0)


def pack_kernel(
    slot, packed_slot, source, records, tails, position, streams, filters, out, facts
):
    write_facts(facts, records, tails, position[0] * BLOCKS)

    def note(unit, carry):
        facts[pl.ds(FROM_PACKED + unit, 1), :] = jnp.full((1, LANES), UNIT * packed_slot[unit], F32)
        facts[pl.ds(FROM_OWN + unit, 1), :] = jnp.full((1, LANES), UNIT * slot[unit], F32)
        return carry

    def note_source(place, carry):
        facts[pl.ds(FROM_BACK + place, 1), :] = jnp.full((1, LANES), UNIT * source[place], F32)
        return carry

    lax.fori_loop(0, UNITS_DEV, note, 0)
    lax.fori_loop(0, SHARDS * CAP, note_source, 0)
    out[...] = jnp.zeros(out.shape, BF16)
    taps = filters[...]
    high, middle, low = parts_of(taps[:, KM:])
    lane = lax.broadcasted_iota(jnp.int32, (8, LANES), 1)
    small = jnp.where(
        lane < 32,
        high,
        jnp.where(
            lane < 64,
            pltpu.roll(middle, 32, 1),
            jnp.where(lane < 96, pltpu.roll(low, 64, 1), 0.0),
        ),
    )
    panel = jnp.concatenate([taps[:, :KM], small], axis=0).astype(BF16)

    def give(shard, carry):
        out[shard, pl.ds(3 * CAP * UNIT, UNIT), :] = panel
        return carry

    lax.fori_loop(0, SHARDS, give, 0)

    def move(unit, carry):
        to = slot[unit]
        shard = to // CAP
        rank = to % CAP
        for s in range(3):
            out[shard, pl.ds(pl.multiple_of((s * CAP + rank) * UNIT, UNIT), UNIT), :] = streams[
                s, pl.ds(pl.multiple_of(unit * UNIT, UNIT), UNIT), :
            ]
        return carry

    lax.fori_loop(0, UNITS_DEV, move, 0)


def unpack_kernel(facts, matrix, arrived, packed, mixer, small, rim, turned):
    for s in range(3):
        packed[s] = pick(matrix[...], slots_of(arrived, s))
    for shard in range(SHARDS):
        panel = arrived[shard, 3 * CAP * UNIT :, :].astype(F32)
        turned[0, shard * 8 : shard * 8 + 8, :] = panel[:8]
        turned[1, shard * 8 : shard * 8 + 8, :] = panel[8:]
    mixer[...] = turned[0].T
    pieces = turned[1].T
    small[...] = pieces[0:32] + pieces[32:64] + pieces[64:96]

    carry = carry_of(facts, BLOCKS - 1)
    live = live_of(facts, BLOCKS - 1)
    heads = lax.broadcasted_iota(jnp.int32, (KM + UNIT, LANES), 0) < UNIT
    keep = jnp.where(heads, carry, 1.0)
    both = []
    for s in (1, 2):
        wide = packed[s, ROWS - KM - UNIT :, :].astype(F32) * keep
        total = jnp.zeros((KM, LANES), F32)
        for tap in range(KF):
            row = tap * 3 + s
            total = total + small[row : row + 1, :] * wide[UNIT - tap : UNIT - tap + KM]
        both.append((total * live).astype(BF16).astype(F32))
    rim[:KM, :] = (both[0] * both[1]).astype(BF16)
    for s in range(3):
        rim[KM + s * UNIT : KM + (s + 1) * UNIT, :] = packed[s, ROWS - UNIT :, :]


def forward_kernel(
    facts,
    packed,
    rim,
    mixer,
    small,
    out_grad,
    feature,
    response,
    sums,
    window,
    mixed,
    pair,
    shifted,
):
    mixed[:KM, :] = rim[:KM, :].astype(F32)
    for b in range(BLOCKS):
        carry = carry_of(facts, b)
        live = live_of(facts, b)
        both = []
        for s in range(3):
            if b == 0:
                tail = rim[KM + s * UNIT : KM + (s + 1) * UNIT, :].astype(F32)
            else:
                tail = packed[s, b * KM - UNIT : b * KM, :].astype(F32)
            window[s, :UNIT, :] = tail * carry
            window[s, UNIT:, :] = packed[s, b * KM : (b + 1) * KM, :].astype(F32)
            total = jnp.zeros((KM, LANES), F32)
            for tap in range(KF):
                row = tap * 3 + s
                total = total + small[row : row + 1, :] * window[s, UNIT - tap : UNIT - tap + KM, :]
            rounded = (total * live).astype(BF16)
            feature[s, b * KM : (b + 1) * KM, :] = rounded
            both.append(rounded.astype(F32))
        mixed[(b + 1) * KM : (b + 2) * KM, :] = (both[1] * both[2]).astype(BF16).astype(F32)

    gain = small[21:22, :]
    ones = jnp.ones((8, LANES), F32)
    line = lax.broadcasted_iota(jnp.int32, (8, LANES), 0)

    def one_block(b, collected):
        carry = carry_of(facts, b)
        here = pl.ds(pl.multiple_of(b * KM, KM), KM)
        pair[:KM, :] = mixed[here, :] * carry
        pair[KM:, :] = mixed[pl.ds(pl.multiple_of((b + 1) * KM, KM), KM), :]
        for s in range(8):
            shifted[s, 8:, :] = pair[8 - s : 2 * KM - s, :]
        total = jnp.zeros((KM, LANES), F32)
        for s in range(8):
            for k in range(16):
                lag = 8 * k + s
                total = total + mixer[lag : lag + 1, :] * shifted[s, KM - 8 * k : 2 * KM - 8 * k, :]
        response[here, :] = total
        gated = (feature[0, here, :].astype(F32) * total).astype(BF16).astype(F32)
        weighted = out_grad[here, :].astype(F32) * gain
        contract = (((1,), (1,)), ((), ()))
        squares = lax.dot_general(
            ones, gated * gated, contract, precision=lax.Precision.HIGHEST,
            preferred_element_type=F32,
        )
        inner = lax.dot_general(
            ones, weighted * gated, contract, precision=lax.Precision.HIGHEST,
            preferred_element_type=F32,
        )
        return jnp.where(line == b, squares, jnp.where(line == b + BLOCKS, inner, collected))

    collected = lax.fori_loop(0, BLOCKS, one_block, jnp.zeros((8, LANES), F32))
    sums[...] = collected


def middle_kernel(
    facts,
    sums,
    feature,
    response,
    mixer,
    small,
    out_grad,
    out,
    query,
    reply,
    gain_sum,
    rim,
    window,
):
    total = jnp.sum(sums[...], axis=0)
    line = lax.broadcasted_iota(jnp.int32, (8, LANES), 0)
    lane = lax.broadcasted_iota(jnp.int32, (8, LANES), 1)
    used = facts[2 * BLOCKS : 4 * BLOCKS, :]
    scale = jnp.where(lane.astype(F32) < used, 1.0, 0.0) * lax.rsqrt(total / C + EPSILON)
    inner = pltpu.roll(total, BLOCKS, 0) * scale / C
    both = jnp.where(line < BLOCKS, scale, pltpu.roll(inner, BLOCKS, 0))
    columns = jnp.concatenate([both] * 16, axis=0).T
    gain = small[21:22, :]
    gain_total = jnp.zeros((8, LANES), F32)
    for b in range(BLOCKS):
        here = slice(b * KM, (b + 1) * KM)
        scale_b = jnp.broadcast_to(columns[:, b : b + 1], (KM, LANES))
        inner_b = jnp.broadcast_to(columns[:, b + BLOCKS : b + BLOCKS + 1], (KM, LANES))
        query_feature = feature[0, here, :].astype(F32)
        answer = response[here, :]
        gated = (query_feature * answer).astype(BF16).astype(F32)
        normed = gated * scale_b
        out[here, :] = (normed * gain).astype(BF16)
        grad = out_grad[here, :].astype(F32)
        gain_total = gain_total + fold8(grad * normed)
        d_gated = (scale_b * (grad * gain - normed * inner_b)).astype(BF16).astype(F32)
        query[here, :] = (d_gated * answer).astype(BF16)
        reply[here, :] = (d_gated * query_feature).astype(BF16)
    gain_sum[...] = gain_total

    carry_next = carry_next_of(facts, 0)
    window[:KM, :] = reply[:KM, :].astype(F32)
    window[KM:, :] = reply[KM : KM + UNIT, :].astype(F32) * carry_next
    totals = [jnp.zeros((8, LANES), F32) for _ in range(4)]
    for lag in range(KM):
        totals[lag % 4] = totals[lag % 4] + mixer[lag : lag + 1, :] * window[lag : lag + 8, :]
    d_mixed = (totals[0] + totals[1]) + (totals[2] + totals[3])
    d_mixed = jnp.concatenate([d_mixed, jnp.zeros_like(d_mixed)], axis=0)
    rim[:KM, :] = reply[:KM, :]
    rim[KM : KM + UNIT, :] = query[:UNIT, :]
    rim[KM + UNIT : KM + 2 * UNIT, :] = (d_mixed * feature[2, :UNIT, :].astype(F32)).astype(BF16)
    rim[KM + 2 * UNIT :, :] = (d_mixed * feature[1, :UNIT, :].astype(F32)).astype(BF16)


def backward_kernel(
    matrix,
    facts,
    query,
    reply,
    rim_back,
    feature,
    packed,
    rim,
    mixer,
    small,
    gain_sum,
    back,
    mixed,
    replies,
    pair,
    shifted,
    lag_total,
    d_feature,
    window,
    tap_total,
    spread,
):
    mixed[:KM, :] = rim[:KM, :].astype(F32)
    replies[ROWS:, :] = rim_back[:KM, :].astype(F32)
    for b in range(BLOCKS):
        here = slice(b * KM, (b + 1) * KM)
        product = feature[1, here, :].astype(F32) * feature[2, here, :].astype(F32)
        mixed[(b + 1) * KM : (b + 2) * KM, :] = product.astype(BF16).astype(F32)
        replies[here, :] = reply[here, :].astype(F32)
    for s in range(3):
        d_feature[s, ROWS:, :] = rim_back[KM + s * UNIT : KM + (s + 1) * UNIT, :].astype(F32)
    d_feature[0, :ROWS, :] = query[...].astype(F32)
    lag_total[...] = jnp.zeros_like(lag_total)

    def one_block(b, unused):
        carry, carry_next = carry_of(facts, b), carry_next_of(facts, b)
        here = pl.ds(pl.multiple_of(b * KM, KM), KM)
        after = pl.ds(pl.multiple_of((b + 1) * KM, KM), KM)
        pair[:KM, :] = replies[here, :]
        pair[KM:, :] = replies[after, :] * carry_next
        for s in range(8):
            shifted[s, : 2 * KM - 8, :] = pair[s : 2 * KM - 8 + s, :]
        total = jnp.zeros((KM, LANES), F32)
        for s in range(8):
            for k in range(16):
                lag = 8 * k + s
                total = total + mixer[lag : lag + 1, :] * shifted[s, 8 * k : 8 * k + KM, :]
        d_feature[1, here, :] = (total * feature[2, here, :].astype(F32)).astype(BF16).astype(F32)
        d_feature[2, here, :] = (total * feature[1, here, :].astype(F32)).astype(BF16).astype(F32)
        pair[:KM, :] = mixed[here, :] * carry
        pair[KM:, :] = mixed[after, :]
        for s in range(8):
            shifted[s, 8:, :] = pair[8 - s : 2 * KM - s, :]
        own = replies[here, :]
        for s in range(8):
            for k in range(16):
                lag = 8 * k + s
                lag_total[lag] = lag_total[lag] + fold8(
                    own * shifted[s, KM - 8 * k : 2 * KM - 8 * k, :]
                )
        return unused

    lax.fori_loop(0, BLOCKS, one_block, 0)

    tap_total[...] = jnp.zeros_like(tap_total)
    for b in range(BLOCKS):
        carry, carry_next = carry_of(facts, b), carry_next_of(facts, b)
        here = slice(b * KM, (b + 1) * KM)
        for s in range(3):
            if b == 0:
                tail = rim[KM + s * UNIT : KM + (s + 1) * UNIT, :].astype(F32)
            else:
                tail = packed[s, b * KM - UNIT : b * KM, :].astype(F32)
            window[:UNIT, :] = tail * carry
            window[UNIT:, :] = packed[s, here, :].astype(F32)
            own = d_feature[s, here, :]
            for tap in range(KF):
                row = tap * 3 + s
                tap_total[row] = tap_total[row] + fold8(own * window[UNIT - tap : UNIT - tap + KM, :])
            window[:KM, :] = own
            window[KM:, :] = d_feature[s, (b + 1) * KM : (b + 1) * KM + UNIT, :] * carry_next
            total = jnp.zeros((KM, LANES), F32)
            for tap in range(KF):
                row = tap * 3 + s
                total = total + small[row : row + 1, :] * window[tap : tap + KM, :]
            spread[s, here, :] = total.astype(BF16)

    tap_total[21] = gain_sum[...]
    mixer_parts = parts_of(jnp.sum(lag_total[...], axis=1).T)
    small_parts = parts_of(jnp.sum(tap_total[...], axis=1))
    rest = jnp.zeros((KM - 96, LANES), F32)
    turned = jnp.concatenate(list(small_parts) + [rest], axis=0).T
    for shard in range(SHARDS):
        rows = slice(shard * 8, shard * 8 + 8)
        pieces = jnp.concatenate([part[rows] for part in mixer_parts] + [turned[rows]], axis=0)
        back[shard, 3 * CAP * UNIT :, :] = pieces.astype(BF16)

    for s in range(3):
        units = pick(matrix[...], spread[s])
        back[:, s * CAP * UNIT : (s + 1) * CAP * UNIT, :] = units.reshape(
            SHARDS, CAP * UNIT, LANES
        )


def finish_kernel(matrix, returned, stream_grad, grads):
    for s in range(3):
        stream_grad[s] = pick(matrix[...], slots_of(returned, s))
    total = jnp.zeros((2 * UNIT, LANES), F32)
    for shard in range(SHARDS):
        total = total + returned[shard, 3 * CAP * UNIT :, :].astype(F32)
    grads[:, :KM] = total[0:8] + total[8:16] + total[16:24]
    pieces = total[24:32]
    grads[:, KM:] = pieces + pltpu.roll(pieces, LANES - 32, 1) + pltpu.roll(pieces, LANES - 64, 1)

MESH = pl.DeviceIdType.MESH


def remote_call(kernel, out_shape, scratch, collective, *operands, scalars=0):
    return pl.pallas_call(
        kernel,
        out_shape=out_shape,
        in_specs=[SMEM] * scalars + [VMEM] * (len(operands) - scalars),
        out_specs=jax.tree.map(lambda _: VMEM, out_shape),
        scratch_shapes=scratch,
        compiler_params=pltpu.CompilerParams(collective_id=collective, has_side_effects=True),
    )(*operands)


def shard_peers():
    member = lax.axis_index("fsdp")
    me = lax.axis_index("seq")
    row, half = me // 2, me % 2
    peers = []
    for away in (1, 7, 2, 6, 3, 5, 4):
        peers.append((row + away) % 8 * 2 + half)
        peers.append((row + away) % 8 * 2 + 1 - half)
    peers.append(row * 2 + 1 - half)
    return member, me, peers


def greet(devices):
    barrier = pltpu.get_barrier_semaphore()
    for device in devices:
        pl.semaphore_signal(barrier, inc=1, device_id=device, device_id_type=MESH)


def met(count):
    pl.semaphore_wait(pltpu.get_barrier_semaphore(), count)


def finish_copies(copies):
    for copy in copies:
        copy.wait_send()
    for copy in copies:
        copy.wait_recv()


def deal(blocks, out, sent, came, own):
    member, me, peers = shard_peers()
    mine = pltpu.make_async_copy(blocks.at[me], out.at[me], own)
    mine.start()
    copies = []
    for number, to in enumerate(peers):
        copy = pltpu.make_async_remote_copy(
            src_ref=blocks.at[to],
            dst_ref=out.at[me],
            send_sem=sent.at[number],
            recv_sem=came.at[number],
            device_id=(member, to),
            device_id_type=MESH,
        )
        copy.start()
        copies.append(copy)
    return mine, copies


def pass_on(source, target, sent, came, by):
    member = lax.axis_index("fsdp")
    to = lax.rem(lax.axis_index("seq") + SHARDS + by, SHARDS)
    copy = pltpu.make_async_remote_copy(
        src_ref=source,
        dst_ref=target,
        send_sem=sent,
        recv_sem=came,
        device_id=(member, to),
        device_id_type=MESH,
    )
    copy.start()
    copy.wait()


def arrive_kernel(
    facts, blocks,
    packed, mixer, small, rim,
    arrived, rim_out, turned, matrix, sent, came, own, rim_sent, rim_came,
):
    member, _, peers = shard_peers()
    greet([(member, to) for to in peers])
    met(len(peers))
    mine, copies = deal(blocks, arrived, sent, came, own)
    one_hot(matrix, facts, FROM_PACKED)
    mine.wait()
    finish_copies(copies)
    unpack_kernel(facts, matrix, arrived, packed, mixer, small, rim_out, turned)
    pass_on(rim_out, rim, rim_sent, rim_came, 1)


def middle_remote_kernel(
    facts, packed, rim, mixer, small, out_grad,
    feature, out, query, reply, gain_sum, rim_back,
    response, collected, sums, rim_out, window3, mixed, pair, shifted, window,
    sent, came, own, rim_sent, rim_came,
):
    members = sums.shape[0]
    member = lax.axis_index("fsdp")
    me = lax.axis_index("seq")
    others = [(lax.rem(member + away, members), me) for away in range(1, members)]
    greet(others + [(member, lax.rem(me + 1, SHARDS))])
    forward_kernel(
        facts, packed, rim, mixer, small, out_grad,
        feature, response, collected, window3, mixed, pair, shifted,
    )
    met(members)
    mine = pltpu.make_async_copy(collected, sums.at[member], own)
    mine.start()
    copies = []
    for number, device in enumerate(others):
        copy = pltpu.make_async_remote_copy(
            src_ref=collected,
            dst_ref=sums.at[member],
            send_sem=sent.at[number],
            recv_sem=came.at[number],
            device_id=device,
            device_id_type=MESH,
        )
        copy.start()
        copies.append(copy)
    mine.wait()
    finish_copies(copies)
    middle_kernel(
        facts, sums, feature, response, mixer, small, out_grad,
        out, query, reply, gain_sum, rim_out, window,
    )
    pass_on(rim_out, rim_back, rim_sent, rim_came, -1)


def return_kernel(
    facts, query, reply, rim_back, feature, packed, rim, mixer, small, gain_sum,
    stream_grad, grads,
    back, returned, mixed, replies, pair, shifted, lag_total, d_feature, window, tap_total,
    spread, to_slots, from_slots, sent, came, own,
):
    member, _, peers = shard_peers()
    greet([(member, to) for to in peers])
    one_hot(to_slots, facts, FROM_BACK)
    backward_kernel(
        to_slots, facts, query, reply, rim_back, feature, packed, rim, mixer, small, gain_sum,
        back, mixed, replies, pair, shifted, lag_total, d_feature, window, tap_total, spread,
    )
    met(len(peers))
    mine, copies = deal(back, returned, sent, came, own)
    one_hot(from_slots, facts, FROM_OWN)
    mine.wait()
    finish_copies(copies)
    finish_kernel(from_slots, returned, stream_grad, grads)


def routing(unit_dest, position):
    target = (unit_dest // UNITS_DEV).reshape(SHARDS, UNITS_DEV)
    ids = jnp.arange(UNITS_DEV, dtype=jnp.int32)
    same = (target[:, :, None] == target[:, None, :]) & (ids[None, :] < ids[:, None])[None]
    rank = jnp.sum(same.astype(jnp.int32), axis=2)
    own_slot = lax.dynamic_index_in_dim(target * CAP + rank, position, 0, keepdims=False)
    arrive = (jnp.arange(SHARDS, dtype=jnp.int32)[:, None] * CAP + rank).reshape(-1)
    match = unit_dest[None, :] == (position * UNITS_DEV + ids)[:, None]
    packed_slot = jnp.sum(jnp.where(match, arrive[None, :], 0), axis=1)
    places = jnp.arange(SHARDS * CAP, dtype=jnp.int32)[:, None]
    back_source = jnp.sum(jnp.where(packed_slot[None, :] == places, ids[None, :], 0), axis=1)
    return own_slot, packed_slot, back_source


def body(
    streams, record_blocks, tail_rows, unit_dest, mixer_filter, feat_filter, norm_gain, out_grad
):
    members = lax.axis_size("fsdp")
    position = lax.axis_index("seq").astype(jnp.int32)
    own_slot, packed_slot, back_source = routing(unit_dest, position)
    where = position.reshape(1)
    filters = jnp.concatenate(
        [
            mixer_filter,
            feat_filter.reshape(KF * 3, 8),
            norm_gain.reshape(1, 8),
            jnp.zeros((LANES - KF * 3 - 1, 8), F32),
        ],
        axis=0,
    ).T
    outgoing, facts = call(
        pack_kernel,
        (shape(SHARDS, OUT_UNITS * UNIT, LANES), shape(FACTS, LANES, dtype=F32)),
        [],
        own_slot,
        packed_slot,
        back_source,
        record_blocks,
        tail_rows,
        where,
        streams,
        filters,
        scalars=6,
    )
    pair_sems = [
        pltpu.SemaphoreType.DMA((SHARDS,)),
        pltpu.SemaphoreType.DMA((SHARDS,)),
        pltpu.SemaphoreType.DMA,
    ]
    packed, mixer, small, rim = remote_call(
        arrive_kernel,
        (
            shape(3, ROWS, LANES),
            shape(KM, LANES, dtype=F32),
            shape(32, LANES, dtype=F32),
            shape(RIM, LANES),
        ),
        [
            pltpu.VMEM(outgoing.shape, BF16),
            pltpu.VMEM((RIM, LANES), BF16),
            pltpu.VMEM((2, LANES, LANES), F32),
            pltpu.VMEM((ROWS, SLOT_ROWS), BF16),
            *pair_sems,
            pltpu.SemaphoreType.DMA,
            pltpu.SemaphoreType.DMA,
        ],
        0,
        facts,
        outgoing,
    )
    feature, out, query, reply, gain_sum, rim_back = remote_call(
        middle_remote_kernel,
        (
            shape(3, ROWS, LANES),
            shape(ROWS, LANES),
            shape(ROWS, LANES),
            shape(ROWS, LANES),
            shape(8, LANES, dtype=F32),
            shape(RIM, LANES),
        ),
        [
            pltpu.VMEM((ROWS, LANES), F32),
            pltpu.VMEM((8, LANES), F32),
            pltpu.VMEM((members, 8, LANES), F32),
            pltpu.VMEM((RIM, LANES), BF16),
            pltpu.VMEM((3, UNIT + KM, LANES), F32),
            pltpu.VMEM((ROWS + KM, LANES), F32),
            pltpu.VMEM((2 * KM, LANES), F32),
            pltpu.VMEM((8, 2 * KM, LANES), F32),
            pltpu.VMEM((KM + UNIT, LANES), F32),
            pltpu.SemaphoreType.DMA((members,)),
            pltpu.SemaphoreType.DMA((members,)),
            pltpu.SemaphoreType.DMA,
            pltpu.SemaphoreType.DMA,
            pltpu.SemaphoreType.DMA,
        ],
        1,
        facts,
        packed,
        rim,
        mixer,
        small,
        out_grad,
    )
    stream_grad, grads = remote_call(
        return_kernel,
        (shape(3, ROWS, LANES), shape(8, 2 * LANES, dtype=F32)),
        [
            pltpu.VMEM((SHARDS, BACK_UNITS * UNIT, LANES), BF16),
            pltpu.VMEM((SHARDS, BACK_UNITS * UNIT, LANES), BF16),
            pltpu.VMEM((ROWS + KM, LANES), F32),
            pltpu.VMEM((ROWS + KM, LANES), F32),
            pltpu.VMEM((2 * KM, LANES), F32),
            pltpu.VMEM((8, 2 * KM, LANES), F32),
            pltpu.VMEM((KM, 8, LANES), F32),
            pltpu.VMEM((3, ROWS + UNIT, LANES), F32),
            pltpu.VMEM((KM + UNIT, LANES), F32),
            pltpu.VMEM((32, 8, LANES), F32),
            pltpu.VMEM((3, ROWS, LANES), BF16),
            pltpu.VMEM((SLOT_ROWS, ROWS), BF16),
            pltpu.VMEM((ROWS, SLOT_ROWS), BF16),
            *pair_sems,
        ],
        2,
        facts,
        query,
        reply,
        rim_back,
        feature,
        packed,
        rim,
        mixer,
        small,
        gain_sum,
    )
    turned = grads.T
    mixer_grad = turned[:KM]
    feat_grad = turned[KM : KM + KF * 3].reshape(KF, 3, 8)
    gain_grad = turned[KM + KF * 3]
    return (out, stream_grad, mixer_grad, feat_grad, gain_grad)


def solution(mesh):
    placed = (
        P(None, "seq", "fsdp"),
        P(),
        P(),
        P(),
        P(None, ("fsdp", "seq")),
        P(None, None, ("fsdp", "seq")),
        P(("fsdp", "seq")),
        P("seq", "fsdp"),
    )
    return jax.shard_map(
        body,
        mesh=mesh,
        in_specs=placed,
        out_specs=(
            P("seq", "fsdp"),
            P(None, "seq", "fsdp"),
            P(None, ("fsdp", "seq")),
            P(None, None, ("fsdp", "seq")),
            P(("fsdp", "seq")),
        ),
        check_vma=False,
    )
```

```python
import functools

import jax
import jax.numpy as jnp
from jax import lax
from jax.experimental import pallas as pl
from jax.experimental.pallas import tpu as pltpu
from jax.sharding import PartitionSpec as P

C = 4096
KM = 128
KF = 7
UNIT = 16
CAP = 4
EPSILON = 1e-06
INTERPRET = False

F32 = jnp.float32
BF16 = jnp.bfloat16
VMEM = pl.BlockSpec(memory_space=pltpu.VMEM)
SMEM = pl.BlockSpec(memory_space=pltpu.SMEM)

LANES = 128
BLOCKS = 4
ROWS = BLOCKS * KM
SHARDS = 16
UNITS_DEV = ROWS // UNIT
OUT_UNITS = 3 * CAP + 1
BACK_UNITS = 3 * CAP + 2
RIM = KM + 3 * UNIT
FROM_PACKED = 16
FROM_OWN = FROM_PACKED + UNITS_DEV
FROM_BACK = FROM_OWN + UNITS_DEV
FACTS = FROM_BACK + SHARDS * CAP
SLOT_ROWS = SHARDS * CAP * UNIT


def call(kernel, out_shape, scratch, *operands, scalars=0):
    return pl.pallas_call(
        kernel,
        out_shape=out_shape,
        in_specs=[SMEM] * scalars + [VMEM] * (len(operands) - scalars),
        out_specs=jax.tree.map(lambda _: VMEM, out_shape),
        scratch_shapes=scratch,
        interpret=INTERPRET,
    )(*operands)


def shape(*dims, dtype=BF16):
    return jax.ShapeDtypeStruct(dims, dtype)


def parts_of(value):
    high = value.astype(BF16).astype(F32)
    rest = value - high
    middle = rest.astype(BF16).astype(F32)
    return high, middle, rest - middle


def block_facts(records, tails, block):
    second = records[0]
    third = records[0] + records[1]
    end = third + records[2]

    def begins(index):
        return (index == 0) | (index == second) | (index == third)

    used = jnp.where(
        block + 1 == second,
        tails[0],
        jnp.where(block + 1 == third, tails[1], jnp.where(block + 1 == end, tails[2], KM)),
    )
    carry = jnp.where(begins(block), 0.0, 1.0).astype(F32)
    carry_next = jnp.where(begins(block + 1) | (block + 1 == end), 0.0, 1.0).astype(F32)
    return carry, carry_next, used


def write_facts(facts, records, tails, first):
    line = lax.broadcasted_iota(jnp.int32, (16, LANES), 0)
    rows = jnp.zeros((16, LANES), F32)
    for b in range(BLOCKS):
        carry, carry_next, used = block_facts(records, tails, first + b)
        rows = jnp.where(line == b, carry, rows)
        rows = jnp.where(line == b + BLOCKS, carry_next, rows)
        rows = jnp.where(line == b + 2 * BLOCKS, used.astype(F32), rows)
    facts[:16, :] = rows


def carry_of(facts, b):
    return facts[pl.ds(b, 1), :]


def carry_next_of(facts, b):
    return facts[pl.ds(b + BLOCKS, 1), :]


def live_of(facts, b):
    rows = lax.broadcasted_iota(jnp.int32, (KM, LANES), 0).astype(F32)
    return jnp.where(rows < facts[pl.ds(b + 2 * BLOCKS, 1), :], 1.0, 0.0)


def one_hot(matrix, facts, base):
    lanes = lax.broadcasted_iota(jnp.int32, (UNIT, LANES), 1)
    rows = lax.broadcasted_iota(jnp.int32, (UNIT, LANES), 0)
    offset = (lanes - rows).astype(F32)

    def unit_rows(unit, carry):
        start = facts[pl.ds(base + unit, 1), :]
        at = pl.ds(pl.multiple_of(unit * UNIT, UNIT), UNIT)
        for column in range(0, matrix.shape[1], LANES):
            picked = jnp.where(offset + column == start, 1.0, 0.0)
            matrix[at, column : column + LANES] = picked.astype(BF16)
        return carry

    lax.fori_loop(0, matrix.shape[0] // UNIT, unit_rows, 0)


def pick(matrix, table):
    return jnp.dot(matrix, table, preferred_element_type=F32).astype(BF16)


def slots_of(arrived, s):
    part = arrived[:, s * CAP * UNIT : (s + 1) * CAP * UNIT, :]
    return part.reshape(SLOT_ROWS, LANES)


def fold8(value):
    return jnp.sum(value.reshape(-1, 8, LANES), axis=0)


def pack_kernel(
    slot, packed_slot, source, records, tails, position, streams, filters, out, facts
):
    write_facts(facts, records, tails, position[0] * BLOCKS)

    def note(unit, carry):
        facts[pl.ds(FROM_PACKED + unit, 1), :] = jnp.full((1, LANES), UNIT * packed_slot[unit], F32)
        facts[pl.ds(FROM_OWN + unit, 1), :] = jnp.full((1, LANES), UNIT * slot[unit], F32)
        return carry

    def note_source(place, carry):
        facts[pl.ds(FROM_BACK + place, 1), :] = jnp.full((1, LANES), UNIT * source[place], F32)
        return carry

    lax.fori_loop(0, UNITS_DEV, note, 0)
    lax.fori_loop(0, SHARDS * CAP, note_source, 0)
    out[...] = jnp.zeros(out.shape, BF16)
    taps = filters[...]
    high, middle, low = parts_of(taps[:, KM:])
    lane = lax.broadcasted_iota(jnp.int32, (8, LANES), 1)
    small = jnp.where(
        lane < 32,
        high,
        jnp.where(
            lane < 64,
            pltpu.roll(middle, 32, 1),
            jnp.where(lane < 96, pltpu.roll(low, 64, 1), 0.0),
        ),
    )
    panel = jnp.concatenate([taps[:, :KM], small], axis=0).astype(BF16)

    def give(shard, carry):
        out[shard, pl.ds(3 * CAP * UNIT, UNIT), :] = panel
        return carry

    lax.fori_loop(0, SHARDS, give, 0)

    def move(unit, carry):
        to = slot[unit]
        shard = to // CAP
        rank = to % CAP
        for s in range(3):
            out[shard, pl.ds(pl.multiple_of((s * CAP + rank) * UNIT, UNIT), UNIT), :] = streams[
                s, pl.ds(pl.multiple_of(unit * UNIT, UNIT), UNIT), :
            ]
        return carry

    lax.fori_loop(0, UNITS_DEV, move, 0)


def unpack_kernel(facts, matrix, arrived, packed, mixer, small, rim, turned):
    for s in range(3):
        packed[s] = pick(matrix[...], slots_of(arrived, s))
    for shard in range(SHARDS):
        panel = arrived[shard, 3 * CAP * UNIT :, :].astype(F32)
        turned[0, shard * 8 : shard * 8 + 8, :] = panel[:8]
        turned[1, shard * 8 : shard * 8 + 8, :] = panel[8:]
    mixer[...] = turned[0].T
    pieces = turned[1].T
    small[...] = pieces[0:32] + pieces[32:64] + pieces[64:96]

    carry = carry_of(facts, BLOCKS - 1)
    live = live_of(facts, BLOCKS - 1)
    heads = lax.broadcasted_iota(jnp.int32, (KM + UNIT, LANES), 0) < UNIT
    keep = jnp.where(heads, carry, 1.0)
    both = []
    for s in (1, 2):
        wide = packed[s, ROWS - KM - UNIT :, :].astype(F32) * keep
        total = jnp.zeros((KM, LANES), F32)
        for tap in range(KF):
            row = tap * 3 + s
            total = total + small[row : row + 1, :] * wide[UNIT - tap : UNIT - tap + KM]
        both.append((total * live).astype(BF16).astype(F32))
    rim[:KM, :] = (both[0] * both[1]).astype(BF16)
    for s in range(3):
        rim[KM + s * UNIT : KM + (s + 1) * UNIT, :] = packed[s, ROWS - UNIT :, :]


def forward_kernel(
    facts,
    packed,
    rim,
    mixer,
    small,
    out_grad,
    feature,
    response,
    sums,
    window,
    mixed,
    pair,
    shifted,
):
    mixed[:KM, :] = rim[:KM, :].astype(F32)
    for b in range(BLOCKS):
        carry = carry_of(facts, b)
        live = live_of(facts, b)
        both = []
        for s in range(3):
            if b == 0:
                tail = rim[KM + s * UNIT : KM + (s + 1) * UNIT, :].astype(F32)
            else:
                tail = packed[s, b * KM - UNIT : b * KM, :].astype(F32)
            window[s, :UNIT, :] = tail * carry
            window[s, UNIT:, :] = packed[s, b * KM : (b + 1) * KM, :].astype(F32)
            total = jnp.zeros((KM, LANES), F32)
            for tap in range(KF):
                row = tap * 3 + s
                total = total + small[row : row + 1, :] * window[s, UNIT - tap : UNIT - tap + KM, :]
            rounded = (total * live).astype(BF16)
            feature[s, b * KM : (b + 1) * KM, :] = rounded
            both.append(rounded.astype(F32))
        mixed[(b + 1) * KM : (b + 2) * KM, :] = (both[1] * both[2]).astype(BF16).astype(F32)

    gain = small[21:22, :]
    ones = jnp.ones((8, LANES), F32)
    line = lax.broadcasted_iota(jnp.int32, (8, LANES), 0)

    def one_block(b, collected):
        carry = carry_of(facts, b)
        here = pl.ds(pl.multiple_of(b * KM, KM), KM)
        pair[:KM, :] = mixed[here, :] * carry
        pair[KM:, :] = mixed[pl.ds(pl.multiple_of((b + 1) * KM, KM), KM), :]
        for s in range(8):
            shifted[s, 8:, :] = pair[8 - s : 2 * KM - s, :]
        total = jnp.zeros((KM, LANES), F32)
        for s in range(8):
            for k in range(16):
                lag = 8 * k + s
                total = total + mixer[lag : lag + 1, :] * shifted[s, KM - 8 * k : 2 * KM - 8 * k, :]
        response[here, :] = total
        gated = (feature[0, here, :].astype(F32) * total).astype(BF16).astype(F32)
        weighted = out_grad[here, :].astype(F32) * gain
        contract = (((1,), (1,)), ((), ()))
        squares = lax.dot_general(
            ones, gated * gated, contract, precision=lax.Precision.HIGHEST,
            preferred_element_type=F32,
        )
        inner = lax.dot_general(
            ones, weighted * gated, contract, precision=lax.Precision.HIGHEST,
            preferred_element_type=F32,
        )
        return jnp.where(line == b, squares, jnp.where(line == b + BLOCKS, inner, collected))

    collected = lax.fori_loop(0, BLOCKS, one_block, jnp.zeros((8, LANES), F32))
    sums[...] = collected


def middle_kernel(
    facts,
    sums,
    feature,
    response,
    mixer,
    small,
    out_grad,
    out,
    query,
    reply,
    gain_sum,
    rim,
    window,
):
    total = jnp.sum(sums[...], axis=0)
    line = lax.broadcasted_iota(jnp.int32, (8, LANES), 0)
    lane = lax.broadcasted_iota(jnp.int32, (8, LANES), 1)
    used = facts[2 * BLOCKS : 4 * BLOCKS, :]
    scale = jnp.where(lane.astype(F32) < used, 1.0, 0.0) * lax.rsqrt(total / C + EPSILON)
    inner = pltpu.roll(total, BLOCKS, 0) * scale / C
    both = jnp.where(line < BLOCKS, scale, pltpu.roll(inner, BLOCKS, 0))
    columns = jnp.concatenate([both] * 16, axis=0).T
    gain = small[21:22, :]
    gain_total = jnp.zeros((8, LANES), F32)
    for b in range(BLOCKS):
        here = slice(b * KM, (b + 1) * KM)
        scale_b = jnp.broadcast_to(columns[:, b : b + 1], (KM, LANES))
        inner_b = jnp.broadcast_to(columns[:, b + BLOCKS : b + BLOCKS + 1], (KM, LANES))
        query_feature = feature[0, here, :].astype(F32)
        answer = response[here, :]
        gated = (query_feature * answer).astype(BF16).astype(F32)
        normed = gated * scale_b
        out[here, :] = (normed * gain).astype(BF16)
        grad = out_grad[here, :].astype(F32)
        gain_total = gain_total + fold8(grad * normed)
        d_gated = (scale_b * (grad * gain - normed * inner_b)).astype(BF16).astype(F32)
        query[here, :] = (d_gated * answer).astype(BF16)
        reply[here, :] = (d_gated * query_feature).astype(BF16)
    gain_sum[...] = gain_total

    carry_next = carry_next_of(facts, 0)
    window[:KM, :] = reply[:KM, :].astype(F32)
    window[KM:, :] = reply[KM : KM + UNIT, :].astype(F32) * carry_next
    totals = [jnp.zeros((8, LANES), F32) for _ in range(4)]
    for lag in range(KM):
        totals[lag % 4] = totals[lag % 4] + mixer[lag : lag + 1, :] * window[lag : lag + 8, :]
    d_mixed = (totals[0] + totals[1]) + (totals[2] + totals[3])
    d_mixed = jnp.concatenate([d_mixed, jnp.zeros_like(d_mixed)], axis=0)
    rim[:KM, :] = reply[:KM, :]
    rim[KM : KM + UNIT, :] = query[:UNIT, :]
    rim[KM + UNIT : KM + 2 * UNIT, :] = (d_mixed * feature[2, :UNIT, :].astype(F32)).astype(BF16)
    rim[KM + 2 * UNIT :, :] = (d_mixed * feature[1, :UNIT, :].astype(F32)).astype(BF16)


def backward_kernel(
    early,
    matrix,
    facts,
    query,
    reply,
    rim_back,
    feature,
    packed,
    rim,
    mixer,
    small,
    gain_sum,
    back,
    mixed,
    replies,
    pair,
    shifted,
    lag_total,
    d_feature,
    window,
    tap_total,
    spread,
):
    mixed[:KM, :] = rim[:KM, :].astype(F32)
    replies[ROWS:, :] = rim_back[:KM, :].astype(F32)
    for b in range(BLOCKS):
        here = slice(b * KM, (b + 1) * KM)
        product = feature[1, here, :].astype(F32) * feature[2, here, :].astype(F32)
        mixed[(b + 1) * KM : (b + 2) * KM, :] = product.astype(BF16).astype(F32)
        replies[here, :] = reply[here, :].astype(F32)
    for s in range(3):
        d_feature[s, ROWS:, :] = rim_back[KM + s * UNIT : KM + (s + 1) * UNIT, :].astype(F32)
    d_feature[0, :ROWS, :] = query[...].astype(F32)
    lag_total[...] = jnp.zeros_like(lag_total)
    tap_total[...] = jnp.zeros_like(tap_total)

    def one_field(s):
        for b in range(BLOCKS):
            carry, carry_next = carry_of(facts, b), carry_next_of(facts, b)
            here = slice(b * KM, (b + 1) * KM)
            if b == 0:
                tail = rim[KM + s * UNIT : KM + (s + 1) * UNIT, :].astype(F32)
            else:
                tail = packed[s, b * KM - UNIT : b * KM, :].astype(F32)
            window[:UNIT, :] = tail * carry
            window[UNIT:, :] = packed[s, here, :].astype(F32)
            own = d_feature[s, here, :]
            for tap in range(KF):
                row = tap * 3 + s
                tap_total[row] = tap_total[row] + fold8(own * window[UNIT - tap : UNIT - tap + KM, :])
            window[:KM, :] = own
            window[KM:, :] = d_feature[s, (b + 1) * KM : (b + 1) * KM + UNIT, :] * carry_next
            total = jnp.zeros((KM, LANES), F32)
            for tap in range(KF):
                row = tap * 3 + s
                total = total + small[row : row + 1, :] * window[tap : tap + KM, :]
            spread[s, here, :] = total.astype(BF16)
        units = pick(matrix[...], spread[s])
        back[:, s * CAP * UNIT : (s + 1) * CAP * UNIT, :] = units.reshape(
            SHARDS, CAP * UNIT, LANES
        )

    def mixed_block(b, unused):
        carry_next = carry_next_of(facts, b)
        here = pl.ds(pl.multiple_of(b * KM, KM), KM)
        after = pl.ds(pl.multiple_of((b + 1) * KM, KM), KM)
        pair[:KM, :] = replies[here, :]
        pair[KM:, :] = replies[after, :] * carry_next
        for s in range(8):
            shifted[s, : 2 * KM - 8, :] = pair[s : 2 * KM - 8 + s, :]
        total = jnp.zeros((KM, LANES), F32)
        for s in range(8):
            for k in range(16):
                lag = 8 * k + s
                total = total + mixer[lag : lag + 1, :] * shifted[s, 8 * k : 8 * k + KM, :]
        d_feature[1, here, :] = (total * feature[2, here, :].astype(F32)).astype(BF16).astype(F32)
        d_feature[2, here, :] = (total * feature[1, here, :].astype(F32)).astype(BF16).astype(F32)
        return unused

    def lag_block(b, unused):
        carry = carry_of(facts, b)
        here = pl.ds(pl.multiple_of(b * KM, KM), KM)
        after = pl.ds(pl.multiple_of((b + 1) * KM, KM), KM)
        pair[:KM, :] = mixed[here, :] * carry
        pair[KM:, :] = mixed[after, :]
        for s in range(8):
            shifted[s, 8:, :] = pair[8 - s : 2 * KM - s, :]
        own = replies[here, :]
        for s in range(8):
            for k in range(16):
                lag = 8 * k + s
                lag_total[lag] = lag_total[lag] + fold8(
                    own * shifted[s, KM - 8 * k : 2 * KM - 8 * k, :]
                )
        return unused

    one_field(0)
    lax.fori_loop(0, BLOCKS, mixed_block, 0)
    early()
    lax.fori_loop(0, BLOCKS, lag_block, 0)
    one_field(1)
    one_field(2)

    tap_total[21] = gain_sum[...]
    mixer_parts = parts_of(jnp.sum(lag_total[...], axis=1).T)
    small_parts = parts_of(jnp.sum(tap_total[...], axis=1))
    rest = jnp.zeros((KM - 96, LANES), F32)
    turned = jnp.concatenate(list(small_parts) + [rest], axis=0).T
    for shard in range(SHARDS):
        rows = slice(shard * 8, shard * 8 + 8)
        pieces = jnp.concatenate([part[rows] for part in mixer_parts] + [turned[rows]], axis=0)
        back[shard, 3 * CAP * UNIT :, :] = pieces.astype(BF16)


def finish_kernel(matrix, returned, stream_grad, grads):
    for s in range(3):
        stream_grad[s] = pick(matrix[...], slots_of(returned, s))
    total = jnp.zeros((2 * UNIT, LANES), F32)
    for shard in range(SHARDS):
        total = total + returned[shard, 3 * CAP * UNIT :, :].astype(F32)
    grads[:, :KM] = total[0:8] + total[8:16] + total[16:24]
    pieces = total[24:32]
    grads[:, KM:] = pieces + pltpu.roll(pieces, LANES - 32, 1) + pltpu.roll(pieces, LANES - 64, 1)

MESH = pl.DeviceIdType.MESH


def remote_call(kernel, out_shape, scratch, collective, *operands, scalars=0):
    return pl.pallas_call(
        kernel,
        out_shape=out_shape,
        in_specs=[SMEM] * scalars + [VMEM] * (len(operands) - scalars),
        out_specs=jax.tree.map(lambda _: VMEM, out_shape),
        scratch_shapes=scratch,
        compiler_params=pltpu.CompilerParams(collective_id=collective, has_side_effects=True),
    )(*operands)


def shard_peers():
    member = lax.axis_index("fsdp")
    me = lax.axis_index("seq")
    row, half = me // 2, me % 2
    peers = []
    for away in (1, 7, 2, 6, 3, 5, 4):
        peers.append((row + away) % 8 * 2 + half)
        peers.append((row + away) % 8 * 2 + 1 - half)
    peers.append(row * 2 + 1 - half)
    return member, me, peers


def greet(devices):
    barrier = pltpu.get_barrier_semaphore()
    for device in devices:
        pl.semaphore_signal(barrier, inc=1, device_id=device, device_id_type=MESH)


def met(count):
    pl.semaphore_wait(pltpu.get_barrier_semaphore(), count)


def finish_copies(copies):
    for copy in copies:
        copy.wait_send()
    for copy in copies:
        copy.wait_recv()


def deal(blocks, out, sent, came, own, rows=slice(None)):
    member, me, peers = shard_peers()
    mine = pltpu.make_async_copy(blocks.at[me, rows], out.at[me, rows], own)
    mine.start()
    copies = []
    for number, to in enumerate(peers):
        copy = pltpu.make_async_remote_copy(
            src_ref=blocks.at[to, rows],
            dst_ref=out.at[me, rows],
            send_sem=sent.at[number],
            recv_sem=came.at[number],
            device_id=(member, to),
            device_id_type=MESH,
        )
        copy.start()
        copies.append(copy)
    return mine, copies


def pass_on(source, target, sent, came, by):
    member = lax.axis_index("fsdp")
    to = lax.rem(lax.axis_index("seq") + SHARDS + by, SHARDS)
    copy = pltpu.make_async_remote_copy(
        src_ref=source,
        dst_ref=target,
        send_sem=sent,
        recv_sem=came,
        device_id=(member, to),
        device_id_type=MESH,
    )
    copy.start()
    copy.wait()


def arrive_kernel(
    facts, blocks,
    packed, mixer, small, rim,
    arrived, rim_out, turned, matrix, sent, came, own, rim_sent, rim_came,
):
    member, _, peers = shard_peers()
    greet([(member, to) for to in peers])
    met(len(peers))
    mine, copies = deal(blocks, arrived, sent, came, own)
    one_hot(matrix, facts, FROM_PACKED)
    mine.wait()
    finish_copies(copies)
    unpack_kernel(facts, matrix, arrived, packed, mixer, small, rim_out, turned)
    pass_on(rim_out, rim, rim_sent, rim_came, 1)


def middle_remote_kernel(
    facts, packed, rim, mixer, small, out_grad,
    feature, out, query, reply, gain_sum, rim_back,
    response, collected, sums, rim_out, window3, mixed, pair, shifted, window,
    sent, came, own, rim_sent, rim_came,
):
    members = sums.shape[0]
    member = lax.axis_index("fsdp")
    me = lax.axis_index("seq")
    others = [(lax.rem(member + away, members), me) for away in range(1, members)]
    greet(others + [(member, lax.rem(me + 1, SHARDS))])
    forward_kernel(
        facts, packed, rim, mixer, small, out_grad,
        feature, response, collected, window3, mixed, pair, shifted,
    )
    met(members)
    mine = pltpu.make_async_copy(collected, sums.at[member], own)
    mine.start()
    copies = []
    for number, device in enumerate(others):
        copy = pltpu.make_async_remote_copy(
            src_ref=collected,
            dst_ref=sums.at[member],
            send_sem=sent.at[number],
            recv_sem=came.at[number],
            device_id=device,
            device_id_type=MESH,
        )
        copy.start()
        copies.append(copy)
    mine.wait()
    finish_copies(copies)
    middle_kernel(
        facts, sums, feature, response, mixer, small, out_grad,
        out, query, reply, gain_sum, rim_out, window,
    )
    pass_on(rim_out, rim_back, rim_sent, rim_came, -1)


def return_kernel(
    facts, query, reply, rim_back, feature, packed, rim, mixer, small, gain_sum,
    stream_grad, grads,
    back, returned, mixed, replies, pair, shifted, lag_total, d_feature, window, tap_total,
    spread, to_slots, from_slots, sent, came, own,
):
    member, _, peers = shard_peers()
    greet([(member, to) for to in peers])
    one_hot(to_slots, facts, FROM_BACK)
    first, rest = slice(0, CAP * UNIT), slice(CAP * UNIT, BACK_UNITS * UNIT)
    pending = []

    def early():
        met(len(peers))
        pending.append(deal(back, returned, sent.at[0], came.at[0], own.at[0], first))

    backward_kernel(
        early, to_slots, facts, query, reply, rim_back, feature, packed, rim, mixer, small,
        gain_sum, back, mixed, replies, pair, shifted, lag_total, d_feature, window, tap_total,
        spread,
    )
    pending.append(deal(back, returned, sent.at[1], came.at[1], own.at[1], rest))
    one_hot(from_slots, facts, FROM_OWN)
    for mine, copies in pending:
        mine.wait()
        finish_copies(copies)
    finish_kernel(from_slots, returned, stream_grad, grads)


def routing(unit_dest, position):
    target = (unit_dest // UNITS_DEV).reshape(SHARDS, UNITS_DEV)
    ids = jnp.arange(UNITS_DEV, dtype=jnp.int32)
    same = (target[:, :, None] == target[:, None, :]) & (ids[None, :] < ids[:, None])[None]
    rank = jnp.sum(same.astype(jnp.int32), axis=2)
    own_slot = lax.dynamic_index_in_dim(target * CAP + rank, position, 0, keepdims=False)
    arrive = (jnp.arange(SHARDS, dtype=jnp.int32)[:, None] * CAP + rank).reshape(-1)
    match = unit_dest[None, :] == (position * UNITS_DEV + ids)[:, None]
    packed_slot = jnp.sum(jnp.where(match, arrive[None, :], 0), axis=1)
    places = jnp.arange(SHARDS * CAP, dtype=jnp.int32)[:, None]
    back_source = jnp.sum(jnp.where(packed_slot[None, :] == places, ids[None, :], 0), axis=1)
    return own_slot, packed_slot, back_source


def body(
    streams, record_blocks, tail_rows, unit_dest, mixer_filter, feat_filter, norm_gain, out_grad
):
    members = lax.axis_size("fsdp")
    position = lax.axis_index("seq").astype(jnp.int32)
    own_slot, packed_slot, back_source = routing(unit_dest, position)
    where = position.reshape(1)
    filters = jnp.concatenate(
        [
            mixer_filter,
            feat_filter.reshape(KF * 3, 8),
            norm_gain.reshape(1, 8),
            jnp.zeros((LANES - KF * 3 - 1, 8), F32),
        ],
        axis=0,
    ).T
    outgoing, facts = call(
        pack_kernel,
        (shape(SHARDS, OUT_UNITS * UNIT, LANES), shape(FACTS, LANES, dtype=F32)),
        [],
        own_slot,
        packed_slot,
        back_source,
        record_blocks,
        tail_rows,
        where,
        streams,
        filters,
        scalars=6,
    )
    pair_sems = [
        pltpu.SemaphoreType.DMA((SHARDS,)),
        pltpu.SemaphoreType.DMA((SHARDS,)),
        pltpu.SemaphoreType.DMA,
    ]
    packed, mixer, small, rim = remote_call(
        arrive_kernel,
        (
            shape(3, ROWS, LANES),
            shape(KM, LANES, dtype=F32),
            shape(32, LANES, dtype=F32),
            shape(RIM, LANES),
        ),
        [
            pltpu.VMEM(outgoing.shape, BF16),
            pltpu.VMEM((RIM, LANES), BF16),
            pltpu.VMEM((2, LANES, LANES), F32),
            pltpu.VMEM((ROWS, SLOT_ROWS), BF16),
            *pair_sems,
            pltpu.SemaphoreType.DMA,
            pltpu.SemaphoreType.DMA,
        ],
        0,
        facts,
        outgoing,
    )
    feature, out, query, reply, gain_sum, rim_back = remote_call(
        middle_remote_kernel,
        (
            shape(3, ROWS, LANES),
            shape(ROWS, LANES),
            shape(ROWS, LANES),
            shape(ROWS, LANES),
            shape(8, LANES, dtype=F32),
            shape(RIM, LANES),
        ),
        [
            pltpu.VMEM((ROWS, LANES), F32),
            pltpu.VMEM((8, LANES), F32),
            pltpu.VMEM((members, 8, LANES), F32),
            pltpu.VMEM((RIM, LANES), BF16),
            pltpu.VMEM((3, UNIT + KM, LANES), F32),
            pltpu.VMEM((ROWS + KM, LANES), F32),
            pltpu.VMEM((2 * KM, LANES), F32),
            pltpu.VMEM((8, 2 * KM, LANES), F32),
            pltpu.VMEM((KM + UNIT, LANES), F32),
            pltpu.SemaphoreType.DMA((members,)),
            pltpu.SemaphoreType.DMA((members,)),
            pltpu.SemaphoreType.DMA,
            pltpu.SemaphoreType.DMA,
            pltpu.SemaphoreType.DMA,
        ],
        1,
        facts,
        packed,
        rim,
        mixer,
        small,
        out_grad,
    )
    stream_grad, grads = remote_call(
        return_kernel,
        (shape(3, ROWS, LANES), shape(8, 2 * LANES, dtype=F32)),
        [
            pltpu.VMEM((SHARDS, BACK_UNITS * UNIT, LANES), BF16),
            pltpu.VMEM((SHARDS, BACK_UNITS * UNIT, LANES), BF16),
            pltpu.VMEM((ROWS + KM, LANES), F32),
            pltpu.VMEM((ROWS + KM, LANES), F32),
            pltpu.VMEM((2 * KM, LANES), F32),
            pltpu.VMEM((8, 2 * KM, LANES), F32),
            pltpu.VMEM((KM, 8, LANES), F32),
            pltpu.VMEM((3, ROWS + UNIT, LANES), F32),
            pltpu.VMEM((KM + UNIT, LANES), F32),
            pltpu.VMEM((32, 8, LANES), F32),
            pltpu.VMEM((3, ROWS, LANES), BF16),
            pltpu.VMEM((SLOT_ROWS, ROWS), BF16),
            pltpu.VMEM((ROWS, SLOT_ROWS), BF16),
            pltpu.SemaphoreType.DMA((2, SHARDS)),
            pltpu.SemaphoreType.DMA((2, SHARDS)),
            pltpu.SemaphoreType.DMA((2,)),
        ],
        2,
        facts,
        query,
        reply,
        rim_back,
        feature,
        packed,
        rim,
        mixer,
        small,
        gain_sum,
    )
    turned = grads.T
    mixer_grad = turned[:KM]
    feat_grad = turned[KM : KM + KF * 3].reshape(KF, 3, 8)
    gain_grad = turned[KM + KF * 3]
    return (out, stream_grad, mixer_grad, feat_grad, gain_grad)


def solution(mesh):
    placed = (
        P(None, "seq", "fsdp"),
        P(),
        P(),
        P(),
        P(None, ("fsdp", "seq")),
        P(None, None, ("fsdp", "seq")),
        P(("fsdp", "seq")),
        P("seq", "fsdp"),
    )
    return jax.shard_map(
        body,
        mesh=mesh,
        in_specs=placed,
        out_specs=(
            P("seq", "fsdp"),
            P(None, "seq", "fsdp"),
            P(None, ("fsdp", "seq")),
            P(None, None, ("fsdp", "seq")),
            P(("fsdp", "seq")),
        ),
        check_vma=False,
    )
```
